256 devices in a mesh: freq: 8 (over x, z_hi), panel: 32 (over z_lo, y, core).
Axes of the slice: x: 4, y: 4, z: 8 (z_hi: 2, z_lo: 4; z = z_hi * 4 + z_lo), core: 2. Of those that a mesh axis runs over, the one named last changes fastest.
Arguments:
- load_history: bfloat16 [4096, 4096], P('freq', 'panel'), may hold values from -6 to 6
- source_blade: int32 [4096], P('panel'), may hold values from 0 to 3
- source_position: float32 [3, 4096], replicated, may hold values from -1 to 1
- airframe_position: float32 [3, 4096], replicated, may hold values from -1 to 1
- airframe_reflect: float32 [4096], P('panel'), may hold values from 0.5 to 2
- observer_position: float32 [3, 4096], replicated, may hold values from -1 to 1
- observer_near: int32 [4096, 4], replicated, may hold values from 0 to 4095
Outputs:
- observer_time: float32 [4096, 4096], P('freq', 'panel')
The draws below stay inside these ranges and needn't reach their ends.
Inputs may be any that keep to these rules, and one draw needn't show every extreme that they name: `observer_near`: an airframe panel may appear more than once in a list.
All inputs are finite; a program needn't handle non-finite values.
Results may differ from the reference program's by a relative error of at most 0.0024.
Values sent between devices are 32-bit elements; how exact they have to be, the bound alone decides.
A program may use at most 64 MiB of HBM per device.

```python
import math
import jax
import jax.numpy as jnp
from jax import lax

TIMES = 4096
FREQS = 128
BLADES = 4
NEAR = 4
SOURCES = 4096
AIRFRAME = 4096
OBSERVERS = 4096


def touch_ends(values, key, least, high):
    longest = values.shape.index(max(values.shape))
    spots = []
    for shift in (0, 1):
        where = [jax.random.randint(jax.random.fold_in(key, axis), (), 0, length) for axis, length in enumerate(values.shape)]
        where[longest] = (where[longest] + shift) % values.shape[longest]
        spots.append(tuple(where))
    return values.at[spots[0]].set(least).at[spots[1]].set(high)


def steps_of(rng, shape, shards, smallest, top_value):
    gain = 1.0
    for dim, shards_of in shards:
        heights = jax.random.uniform(jax.random.fold_in(jax.random.fold_in(rng, 6), dim), (shards_of,), jnp.float32, smallest / len(shards), top_value / len(shards))
        gain = gain * jnp.repeat(jnp.exp(heights), shape[dim] // shards_of).reshape((-1,) + (1,) * (len(shape) - 1 - dim))
    return gain


def noise(own_key, dims, deviation, limit, split=(), kind=jnp.bfloat16):
    drawn = deviation * jax.random.normal(own_key, dims, jnp.float32)
    if split:
        drawn = drawn * steps_of(own_key, dims, split, -0.22, 0.18)
    return jnp.clip(drawn, -limit, limit).astype(kind)


def setup_inputs(seed: int = 0) -> dict:
    splits = jax.random.split(jax.random.key(seed), 8)
    return {
        "load_history": noise(splits[0], (TIMES, SOURCES), 1.0, 6.0, ((0, 8), (1, 32))),
        "source_blade": touch_ends(jax.random.randint(splits[1], (SOURCES,), 0, BLADES), jax.random.fold_in(splits[1], 1), 0, BLADES - 1).astype(jnp.int32),
        "source_position": jnp.clip(jax.random.uniform(splits[2], (3, SOURCES), jnp.float32, -1.0, 1.0), -1.0, 1.0),
        "airframe_position": jnp.clip(jax.random.uniform(splits[3], (3, AIRFRAME), jnp.float32, -1.0, 1.0), -1.0, 1.0),
        "airframe_reflect": jnp.clip(jnp.exp(math.log(2.0) - 1.3862944 * jax.random.uniform(splits[4], (AIRFRAME,), jnp.float32) ** steps_of(splits[4], (AIRFRAME,), ((0, 32),), -0.2, 0.2)), 0.5, 2.0),
        "observer_position": jnp.clip(jax.random.uniform(splits[5], (3, OBSERVERS), jnp.float32, -1.0, 1.0), -1.0, 1.0),
        "observer_near": touch_ends(jax.random.randint(splits[6], (OBSERVERS, NEAR), 0, AIRFRAME), jax.random.fold_in(splits[6], 1), 0, AIRFRAME - 1).astype(jnp.int32),
    }


wave_base = 8.0
wave_step = 0.15
near_gain = 0.5
hub_height = 3.0
ground_depth = -4.0

def lifted(position, height):
    return position + jnp.array([0.0, 0.0, height], jnp.float32)[:, None]

def distances(targets, anchors):
    offset_vec = targets[:, :, None] - anchors[:, None, :]
    return jnp.sqrt(lax.optimization_barrier(jnp.sum(offset_vec * offset_vec, axis=0)))

def radiate(wave_numbers, spread, source):
    inverse = 1.0 / (4.0 * math.pi * spread)
    phase_angle = wave_numbers[:, None, None] * spread[None]
    real_part = jnp.cos(phase_angle) * inverse
    imag_part = -jnp.sin(phase_angle) * inverse
    out_re = lax.optimization_barrier(jnp.sum(real_part * source[0][:, None, :] - imag_part * source[1][:, None, :], axis=2))
    out_im = lax.optimization_barrier(jnp.sum(real_part * source[1][:, None, :] + imag_part * source[0][:, None, :], axis=2))
    return jnp.stack([out_re, out_im])

def radiate_grouped(wave_numbers, spread, source, group_limit):
    freq_total = wave_numbers.shape[0]
    group_size = math.gcd(group_limit, freq_total)
    block_total = freq_total // group_size
    wave_blocks = wave_numbers.reshape(block_total, group_size)
    source_blocks = jnp.moveaxis(source.reshape(2, block_total, group_size, source.shape[2]), 1, 0)
    result = lax.map(lambda entry_pair: radiate(entry_pair[0], spread, entry_pair[1]), (wave_blocks, source_blocks))
    return jnp.moveaxis(result, 0, 1).reshape(2, freq_total, spread.shape[0])

def reference(load_history, source_blade, source_position, airframe_position, airframe_reflect, observer_position, observer_near):
    harmonic = jnp.arange(1, FREQS + 1, dtype=jnp.int32)
    time_steps = jnp.arange(TIMES, dtype=jnp.int32)
    angle_table = (harmonic[:, None] * time_steps[None, :] % TIMES).astype(jnp.float32) * (2.0 * math.pi / TIMES)
    cos_table = jnp.cos(angle_table).astype(jnp.bfloat16)
    sin_table = jnp.sin(angle_table).astype(jnp.bfloat16)
    spectrum_re = jnp.dot(cos_table, load_history, preferred_element_type=jnp.float32) * TIMES ** (-0.5)
    spectrum_im = -jnp.dot(sin_table, load_history, preferred_element_type=jnp.float32) * TIMES ** (-0.5)
    blade_angle = (harmonic[:, None] * source_blade[None, :] % BLADES).astype(jnp.float32) * (2.0 * math.pi / BLADES)
    rotated_re = spectrum_re * jnp.cos(blade_angle) + spectrum_im * jnp.sin(blade_angle)
    rotated_im = spectrum_im * jnp.cos(blade_angle) - spectrum_re * jnp.sin(blade_angle)
    rotated = jnp.stack([rotated_re, rotated_im])
    wave_numbers = wave_base + wave_step * jnp.arange(FREQS, dtype=jnp.int32).astype(jnp.float32)
    incident = radiate_grouped(wave_numbers, distances(airframe_position, lifted(source_position, hub_height)), rotated, 2)
    scattered = incident * airframe_reflect[None, None, :]
    far_field = radiate_grouped(wave_numbers, distances(lifted(observer_position, ground_depth), airframe_position), scattered, 2)
    near_field = lax.optimization_barrier(jnp.sum(scattered[:, :, observer_near], axis=3))
    observed = far_field + near_gain * near_field
    back_cos = jnp.cos(angle_table)
    back_sin = jnp.sin(angle_table)
    series = jnp.dot(back_cos.T, observed[0], precision=lax.Precision.HIGHEST) - jnp.dot(back_sin.T, observed[1], precision=lax.Precision.HIGHEST)
    return series * (2 * FREQS) ** (-0.5)
```

```python
import functools
import math

import jax
import jax.numpy as jnp
import numpy as np
from jax import lax
from jax.experimental import pallas as pl
from jax.experimental.pallas import tpu as pltpu
from jax.sharding import PartitionSpec as P

MESH = pl.DeviceIdType.MESH
F32, BF16 = jnp.float32, jnp.bfloat16
TIMES = 4096
PANELS = 32
LANES = 128
T_DEV = 512
F_DEV = 16
CHUNK = 4 * LANES
ROWS = 64


def fitted(fn, low, high, degree):
    cheb = np.polynomial.chebyshev.Chebyshev.interpolate(fn, degree, [low, high])
    return [float(v) for v in cheb.convert(kind=np.polynomial.Polynomial).coef]


COS_TURN = fitted(lambda u: np.cos(2 * np.pi * np.sqrt(u)), 1e-12, 0.25, 6)
SIN_TURN = fitted(lambda u: np.sin(2 * np.pi * np.sqrt(u)) / np.sqrt(u), 1e-12, 0.25, 5)
COS_HALF = fitted(lambda u: np.cos(0.075 * np.sqrt(u)), 0.99, 44.1, 3)
SIN_HALF = fitted(lambda u: np.sin(0.075 * np.sqrt(u)) / np.sqrt(u), 0.99, 44.1, 3)


def poly(coef, u):
    total = coef[-1] * u + coef[-2]
    for c in coef[-3::-1]:
        total = total * u + c
    return total


def row_freq(row):
    offset, base, side = (row // 8) % 4, (row // 4) % 2, (row // 2) % 2
    return 8 * base + jnp.where(side == 0, 4 + offset, 3 - offset)


def turn_cos(numbers):
    turn = (((numbers + 2048) & 4095) - 2048).astype(F32) * (1.0 / 4096.0)
    return poly(COS_TURN, turn * turn)


def swapped(v, even):
    n = v.shape[0]
    return jnp.where(even, pltpu.roll(v, n - 1, 0), pltpu.roll(v, 1, 0))


def body(
    load_ref, blade_ref, src_ref, air_ref, reflect_ref, obs_ref, near_ref, out_ref,
    table, part, recv_x, own, recv_z, gat1, gat2, spec, state1, state2, hits, back_hi, back_lo,
    column, weights,
    sx, rx, sz, rz, sy1, ry1, sc1, rc1, sl, rl, sy2, ry2, sc2, rc2, sf, rf,
):
    fi, pi = lax.axis_index("freq"), lax.axis_index("panel")
    x, zh = fi // 2, fi % 2
    zl, y, c = pi // 8, (pi // 2) % 4, pi % 2
    z = zh * 4 + zl

    def x_peer(d):
        return (((x + d) % 4) * 2 + zh, pi)

    def z_of(d):
        return (z + d) % 8

    def z_peer(d):
        zz = (z + d) % 8
        return (x * 2 + zz // 4, (zz % 4) * 8 + y * 2 + c)

    def y_peer(d):
        return (fi, zl * 8 + ((y + d) % 4) * 2 + c)

    def line_peer(d):
        return (fi, ((zl + d) % 4) * 8 + y * 2 + c)

    core_peer = (fi, zl * 8 + y * 2 + (1 - c))
    half_peer = (x * 2 + (1 - zh), pi)

    def send(src, dst, ssem, rsem, to):
        return pltpu.make_async_remote_copy(
            src_ref=src, dst_ref=dst, send_sem=ssem, recv_sem=rsem, device_id=to, device_id_type=MESH
        )

    barrier = pltpu.get_barrier_semaphore()
    peers = [x_peer(d) for d in (1, 2, 3)] + [z_peer(d) for d in range(1, 8)]
    peers += [y_peer(d) for d in (1, 2, 3)] + [core_peer]
    for to in peers:
        pl.semaphore_signal(barrier, inc=1, device_id=to, device_id_type=MESH)

    def table_rows(i, _):
        row = lax.broadcasted_iota(jnp.int32, (32, T_DEV), 0)
        t = lax.broadcasted_iota(jnp.int32, (32, T_DEV), 1) + fi * T_DEV
        m = i * F_DEV + row_freq(row) + 1
        table[pl.ds(pl.multiple_of(i * 32, 32), 32), :] = turn_cos(m * t + 1024 * (row % 2)).astype(BF16)
        return 0

    lax.fori_loop(0, 8, table_rows, 0)
    spectrum = jnp.dot(table[...], load_ref[...], preferred_element_type=F32) * (1.0 / 64.0)
    part[...] = spectrum.reshape(4, 64, LANES)

    pl.semaphore_wait(barrier, len(peers))

    x_sends = [
        send(part.at[(x + d) % 4], recv_x.at[d - 1], sx.at[d - 1], rx.at[d - 1], x_peer(d)) for d in (1, 2, 3)
    ]
    for s in x_sends:
        s.start()

    def setup(state, targets, anchors, lift, start, stop):
        wave = (8.0 + 0.15 * (F_DEV * fi.astype(F32) + 7.5)) * (1.0 / (2.0 * math.pi))
        at = pl.multiple_of(pi * LANES, LANES)
        tx, ty, tz = (targets[i : i + 1, pl.ds(at, LANES)] for i in range(3))

        def panel(k, _):
            dc, dy, zz = k // 16, (k // 4) % 4, k % 4
            p = zz * 8 + ((y - dy + 4) % 4) * 2 + (c + dc) % 2
            lane = pl.multiple_of(p * LANES, LANES)
            for i in range(3):
                row = jnp.broadcast_to(anchors[i : i + 1, pl.ds(lane, LANES)], (LANES, LANES))
                column[i] = row.T
            for h in range(LANES // ROWS):
                rows = pl.ds(h * ROWS, ROWS)
                dx, ddy, dz = tx - column[0, rows, :], ty - column[1, rows, :], (tz - lift) - column[2, rows, :]
                square = dx * dx + ddy * ddy + dz * dz
                inverse = lax.rsqrt(square)
                r = square * inverse
                turns = r * wave
                turns = turns - jnp.round(turns)
                u = turns * turns
                gain = inverse * (1.0 / (4.0 * math.pi))
                cp = poly(COS_TURN, u) * gain
                sp = poly(SIN_TURN, u) * turns * gain
                c0 = poly(COS_HALF, square)
                s0 = poly(SIN_HALF, square) * r
                twice = 4.0 * (c0 * c0) - 2.0
                c1, s1 = (twice - 1.0) * c0, (twice + 1.0) * s0
                c2, s2 = twice * c1 - c0, twice * s1 - s0
                c3, s3 = twice * c2 - c1, twice * s2 - s1
                cb, sb = c3 * c0 - s3 * s0, s3 * c0 + c3 * s0
                cc, ss, sc, cs = cp * cb, sp * sb, sp * cb, cp * sb
                dst = pl.ds(pl.multiple_of(k * LANES + h * ROWS, ROWS), ROWS)
                values = (cc + ss, sc - cs, cc - ss, sc + cs, c0, c1, c2, c3, s0, s1, s2, s3)
                for n, v in enumerate(values):
                    state[n, dst, :] = v.astype(BF16)
            return 0

        lax.fori_loop(start, stop, panel, 0)

    setup1 = functools.partial(setup, state1, air_ref, src_ref, 3.0)
    setup2 = functools.partial(setup, state2, obs_ref, air_ref, 4.0)

    setup1(0, 12)

    for s in x_sends:
        s.wait_recv()
    row = lax.broadcasted_iota(jnp.int32, (64, LANES), 0)
    even = row % 2 == 0
    total = part[x] + recv_x[0] + recv_x[1] + recv_x[2]
    quarter = ((row_freq(row) + 1) * blade_ref[...]) & 3
    cos_q = (quarter == 0).astype(F32) - (quarter == 2).astype(F32)
    sin_q = (quarter == 1).astype(F32) - (quarter == 3).astype(F32)
    turned = total * cos_q + swapped(total, even) * jnp.where(even, sin_q, -sin_q)
    own[...] = turned.reshape(2, 32, LANES)
    z_sends = [
        send(own.at[z_of(d) // 4], recv_z.at[z], sz.at[d - 1], rz.at[d - 1], z_peer(d)) for d in range(1, 8)
    ]
    for s in z_sends:
        s.start()
    recv_z[z] = own[zh]

    setup1(12, 32)

    for s in z_sends:
        s.wait_recv()
    gat1[c, y] = recv_z[0:4] + recv_z[4:8]

    def spread(gat, sy, ry, sc, rc):
        y_sends = [send(gat.at[c, y], gat.at[c, y], sy.at[d - 1], ry.at[d - 1], y_peer(d)) for d in (1, 2, 3)]
        for s in y_sends:
            s.start()
        c_sends = [
            send(gat.at[c, (y - d + 4) % 4], gat.at[c, (y - d + 4) % 4], sc.at[d], rc.at[d], core_peer)
            for d in range(4)
        ]
        c_sends[0].start()
        return y_sends, c_sends

    def forward(y_sends, c_sends):
        for d in (1, 2, 3):
            y_sends[d - 1].wait_recv()
            c_sends[d].start()

    y_sends, c_sends = spread(gat1, sy1, ry1, sc1, rc1)
    setup2(0, 12)
    forward(y_sends, c_sends)

    def radiate(gat, state, c_sends, near):
        row = lax.broadcasted_iota(jnp.int32, (32, LANES), 0)
        even = row % 2 == 0
        side = jnp.where((row // 2) % 2 == 0, 1.0, -1.0).astype(F32)
        acc = tuple(jnp.zeros((16, 256), F32) for _ in range(4))
        near_acc = jnp.zeros((64, LANES), F32)
        for dc in range(2):
            for dy in range(4):
                if dc:
                    c_sends[dy].wait_recv()
                cc, yy = (c + dc) % 2, (y - dy + 4) % 4
                for zz in range(4):
                    v = gat[cc, yy, zz]
                    hi = v.astype(BF16).astype(F32)
                    lo = v - hi
                    kinds = []
                    for part_ in (hi, lo):
                        sw = swapped(part_, even)
                        sw = jnp.where(even, sw, -sw)
                        kinds.append((part_, part_ * -side, sw, sw * side))
                    for kind in range(4):
                        for jj in range(4):
                            pair = jnp.concatenate([q[kind][8 * jj : 8 * jj + 8] for q in kinds], axis=0)
                            weights[
                                zz // 2, jj, :, kind * 256 + (zz % 2) * LANES : kind * 256 + (zz % 2 + 1) * LANES
                            ] = pair.astype(BF16)

                def tile(kt, carry):
                    acc, near_acc = carry
                    rows = pl.ds(pl.multiple_of((dc * 4 + dy) * CHUNK + kt * 256, 256), 256)
                    ec0, es0, ec1, es1 = (state[n, rows, :] for n in range(4))
                    new = []
                    for jj in range(4):
                        cj, sj = state[4 + jj, rows, :], state[8 + jj, rows, :]
                        big = jnp.concatenate(
                            [
                                jnp.concatenate([ec0 * cj, ec1 * cj], axis=1),
                                jnp.concatenate([es0 * sj, es1 * sj], axis=1),
                                jnp.concatenate([es0 * cj, es1 * cj], axis=1),
                                jnp.concatenate([ec0 * sj, ec1 * sj], axis=1),
                            ],
                            axis=0,
                        )
                        new.append(acc[jj] + jnp.dot(weights[kt, jj], big, preferred_element_type=F32))
                    if near:
                        left = jnp.concatenate([weights[kt, jj, :, 0:256] for jj in range(4)], axis=0)
                        near_acc = near_acc + jnp.dot(left, hits[rows, :], preferred_element_type=F32)
                    return tuple(new), near_acc

                acc, near_acc = lax.fori_loop(0, 2, tile, (acc, near_acc))
        low = lax.broadcasted_iota(jnp.int32, (8, LANES), 0) < 4
        blocks = []
        for jj in range(4):
            both = acc[jj][0:8] + acc[jj][8:16]
            block = jnp.where(low, both[:, :LANES], both[:, LANES:])
            if near:
                block = block + near_acc[16 * jj : 16 * jj + 8] + near_acc[16 * jj + 8 : 16 * jj + 16]
            blocks.append(block)
        return jnp.concatenate(blocks, axis=0)

    incident = radiate(gat1, state1, c_sends, False)
    gat2[c, y, zl] = incident * reflect_ref[...]
    l_sends = [
        send(gat2.at[c, y, zl], gat2.at[c, y, zl], sl.at[d - 1], rl.at[d - 1], line_peer(d)) for d in (1, 2, 3)
    ]
    for s in l_sends:
        s.start()

    setup2(12, 32)

    for s in l_sends:
        s.wait_recv()
    y_sends2, c_sends2 = spread(gat2, sy2, ry2, sc2, rc2)

    lists = near_ref[:, pl.ds(pl.multiple_of(pi * LANES, LANES), LANES)]

    def count(k, _):
        dc, dy, zz = k // 16, (k // 4) % 4, k % 4
        p = zz * 8 + ((y - dy + 4) % 4) * 2 + (c + dc) % 2
        index = lax.broadcasted_iota(jnp.int32, (LANES, LANES), 0) + p * LANES
        total = jnp.zeros((LANES, LANES), F32)
        for n in range(4):
            total = total + jnp.where(index == lists[n : n + 1, :], 0.5, 0.0)
        hits[pl.ds(pl.multiple_of(k * LANES, LANES), LANES), :] = total.astype(BF16)
        return 0

    lax.fori_loop(0, PANELS, count, 0)

    def back_rows(i, _):
        col = lax.broadcasted_iota(jnp.int32, (32, 256), 1)
        t = lax.broadcasted_iota(jnp.int32, (32, 256), 0) + fi * T_DEV + i * 32
        m = (col // 32) * F_DEV + row_freq(col) + 1
        value = turn_cos(m * t + 1024 * (col % 2))
        hi = value.astype(BF16)
        dst = pl.ds(pl.multiple_of(i * 32, 32), 32)
        back_hi[dst, :] = hi
        back_lo[dst, :] = (value - hi.astype(F32)).astype(BF16)
        return 0

    lax.fori_loop(0, T_DEV // 32, back_rows, 0)

    forward(y_sends2, c_sends2)
    spec[fi] = radiate(gat2, state2, c_sends2, True)

    f_sends = [send(spec.at[fi], spec.at[fi], sf.at[0], rf.at[0], half_peer)]
    f_sends += [send(spec.at[fi], spec.at[fi], sf.at[d], rf.at[d], x_peer(d)) for d in (1, 2, 3)]
    other = x * 2 + (1 - zh)
    f_sends += [send(spec.at[other], spec.at[other], sf.at[3 + d], rf.at[3 + d], x_peer(d)) for d in (1, 2, 3)]
    for s in f_sends[:4]:
        s.start()
    f_sends[0].wait_recv()
    for s in f_sends[4:]:
        s.start()
    for s in f_sends[1:]:
        s.wait_recv()

    observed = spec[...].reshape(256, LANES) * (1.0 / 16.0)
    hi = observed.astype(BF16)
    lo = (observed - hi.astype(F32)).astype(BF16)
    wide = jnp.dot(back_hi[...], jnp.concatenate([hi, lo], axis=1), preferred_element_type=F32)
    narrow = jnp.dot(back_lo[...], hi, preferred_element_type=F32)
    out_ref[...] = wide[:, :LANES] + wide[:, LANES:] + narrow

    for s in x_sends + z_sends + y_sends + c_sends + l_sends + y_sends2 + c_sends2 + f_sends:
        s.wait_send()


def on_device(load, blade, source, airframe, reflect, observer, near):
    vmem = pl.BlockSpec(memory_space=pltpu.VMEM)
    dma = pltpu.SemaphoreType.DMA
    scratch = [
        pltpu.VMEM((256, T_DEV), BF16),
        pltpu.VMEM((4, 64, LANES), F32),
        pltpu.VMEM((3, 64, LANES), F32),
        pltpu.VMEM((2, 32, LANES), F32),
        pltpu.VMEM((8, 32, LANES), F32),
        pltpu.VMEM((2, 4, 4, 32, LANES), F32),
        pltpu.VMEM((2, 4, 4, 32, LANES), F32),
        pltpu.VMEM((8, 32, LANES), F32),
        pltpu.VMEM((12, 4096, LANES), BF16),
        pltpu.VMEM((12, 4096, LANES), BF16),
        pltpu.VMEM((4096, LANES), BF16),
        pltpu.VMEM((T_DEV, 256), BF16),
        pltpu.VMEM((T_DEV, 256), BF16),
        pltpu.VMEM((3, LANES, LANES), F32),
        pltpu.VMEM((2, 4, 16, 1024), BF16),
    ]
    scratch += [dma((n,)) for n in (3, 3, 7, 7, 3, 3, 4, 4, 3, 3, 3, 3, 4, 4, 7, 7)]
    return pl.pallas_call(
        body,
        out_shape=jax.ShapeDtypeStruct((T_DEV, LANES), F32),
        in_specs=[vmem] * 7,
        out_specs=vmem,
        scratch_shapes=scratch,
        compiler_params=pltpu.CompilerParams(
            collective_id=0, has_side_effects=True, vmem_limit_bytes=56 * 1024 * 1024
        ),
        name="rotor",
    )(load, blade.reshape(1, LANES), source, airframe, reflect.reshape(1, LANES), observer, near.T)


def solution(mesh):
    return jax.shard_map(
        on_device,
        mesh=mesh,
        in_specs=(P("freq", "panel"), P("panel"), P(), P(), P("panel"), P(), P()),
        out_specs=P("freq", "panel"),
        check_vma=False,
    )
```

```python
import functools
import math

import jax
import jax.numpy as jnp
import numpy as np
from jax import lax
from jax.experimental import pallas as pl
from jax.experimental.pallas import tpu as pltpu
from jax.sharding import PartitionSpec as P

MESH = pl.DeviceIdType.MESH
F32, BF16 = jnp.float32, jnp.bfloat16
TIMES = 4096
PANELS = 32
LANES = 128
T_DEV = 512
F_DEV = 16
CUT = (20, 8, 24)
ROWS = 64


def fitted(fn, low, high, degree):
    cheb = np.polynomial.chebyshev.Chebyshev.interpolate(fn, degree, [low, high])
    return [float(v) for v in cheb.convert(kind=np.polynomial.Polynomial).coef]


COS_TURN = fitted(lambda u: np.cos(2 * np.pi * np.sqrt(u)), 1e-12, 0.25, 6)
SIN_TURN = fitted(lambda u: np.sin(2 * np.pi * np.sqrt(u)) / np.sqrt(u), 1e-12, 0.25, 5)
COS_HALF = fitted(lambda u: np.cos(0.075 * np.sqrt(u)), 0.99, 44.1, 3)
SIN_HALF = fitted(lambda u: np.sin(0.075 * np.sqrt(u)) / np.sqrt(u), 0.99, 44.1, 3)


def poly(coef, u):
    total = coef[-1] * u + coef[-2]
    for c in coef[-3::-1]:
        total = total * u + c
    return total


def row_freq(row):
    offset, base, side = (row // 8) % 4, (row // 4) % 2, (row // 2) % 2
    return 8 * base + jnp.where(side == 0, 4 + offset, 3 - offset)


def turn_cos(numbers):
    turn = (((numbers + 2048) & 4095) - 2048).astype(F32) * (1.0 / 4096.0)
    return poly(COS_TURN, turn * turn)


def swapped(v, even):
    n = v.shape[0]
    return jnp.where(even, pltpu.roll(v, n - 1, 0), pltpu.roll(v, 1, 0))


def body(
    load_ref, blade_ref, src_ref, air_ref, reflect_ref, obs_ref, near_ref, out_ref,
    part, recv_x, own, recv_z, mine1, recv1, line2, mine2, recv2, spec,
    sx, rx, sz, rz, s1, r1, sl, rl, s2, r2, sf, rf,
):
    fi, pi = lax.axis_index("freq"), lax.axis_index("panel")
    x, zh = fi // 2, fi % 2
    zl, y, c = pi // 8, (pi // 2) % 4, pi % 2
    z = zh * 4 + zl

    def x_peer(d):
        return (((x + d) % 4) * 2 + zh, pi)

    def z_of(d):
        return (z + d) % 8

    def z_peer(d):
        zz = (z + d) % 8
        return (x * 2 + zz // 4, (zz % 4) * 8 + y * 2 + c)

    def line_peer(d):
        return (fi, ((zl + d) % 4) * 8 + y * 2 + c)

    def block_panel(i):
        q = i // 2
        dy = (2 + q + q // 2 + 2 * (q // 3)) % 4
        return zl * 8 + ((y + dy) % 4) * 2 + (c + 1 - i % 2) % 2

    half_peer = (x * 2 + (1 - zh), pi)

    def send(src, dst, ssem, rsem, to):
        return pltpu.make_async_remote_copy(
            src_ref=src, dst_ref=dst, send_sem=ssem, recv_sem=rsem, device_id=to, device_id_type=MESH
        )

    barrier = pltpu.get_barrier_semaphore()
    peers = [x_peer(d) for d in (1, 2, 3)] + [z_peer(d) for d in range(1, 8)]
    peers += [(fi, block_panel(i)) for i in range(7)]
    for to in peers:
        pl.semaphore_signal(barrier, inc=1, device_id=to, device_id_type=MESH)

    def work(table, state1, state2, hits, back_hi, back_lo, column1, column2, weights):
        def table_rows(i, _):
            row = lax.broadcasted_iota(jnp.int32, (32, T_DEV), 0)
            t = lax.broadcasted_iota(jnp.int32, (32, T_DEV), 1) + fi * T_DEV
            m = i * F_DEV + row_freq(row) + 1
            table[pl.ds(pl.multiple_of(i * 32, 32), 32), :] = turn_cos(m * t + 1024 * (row % 2)).astype(BF16)
            return 0

        lax.fori_loop(0, 8, table_rows, 0)
        spectrum = jnp.dot(table[...], load_ref[...], preferred_element_type=F32) * (1.0 / 64.0)
        part[...] = spectrum.reshape(4, 64, LANES)

        def columns(column, anchors):
            def one(zz, _):
                lane = pl.multiple_of((zz * 8 + y * 2 + c) * LANES, LANES)
                for i in range(3):
                    row = jnp.broadcast_to(anchors[i : i + 1, pl.ds(lane, LANES)], (LANES, LANES))
                    column[zz, i] = row.T
                return 0

            lax.fori_loop(0, 4, one, 0)

        wave = (8.0 + 0.15 * (F_DEV * fi.astype(F32) + 7.5)) * (1.0 / (2.0 * math.pi))

        def setup(state, targets, column, lift, start, stop):
            def panel(k, _):
                zz = k % 4
                at = pl.multiple_of(block_panel(k // 4) * LANES, LANES)
                tx, ty, tz = (targets[i : i + 1, pl.ds(at, LANES)] for i in range(3))
                tz = tz - lift
                for h in range(LANES // ROWS):
                    rows = pl.ds(h * ROWS, ROWS)
                    dx, dy, dz = tx - column[zz, 0, rows, :], ty - column[zz, 1, rows, :], tz - column[zz, 2, rows, :]
                    square = dx * dx + dy * dy + dz * dz
                    inverse = lax.rsqrt(square)
                    r = square * inverse
                    turns = r * wave
                    turns = turns - jnp.round(turns)
                    u = turns * turns
                    gain = inverse * (1.0 / (4.0 * math.pi))
                    cp = poly(COS_TURN, u) * gain
                    sp = poly(SIN_TURN, u) * (turns * gain)
                    c0 = poly(COS_HALF, square)
                    s0 = poly(SIN_HALF, square) * r
                    twice = 4.0 * (c0 * c0) - 2.0
                    c1, s1_ = (twice - 1.0) * c0, (twice + 1.0) * s0
                    c2, s2_ = twice * c1 - c0, twice * s1_ - s0
                    c3, s3 = twice * c2 - c1, twice * s2_ - s1_
                    cb, sb = c3 * c0 - s3 * s0, s3 * c0 + c3 * s0
                    cp, sp, cb, sb = (v.astype(BF16) for v in (cp, sp, cb, sb))
                    cc, ss, sc, cs = cp * cb, sp * sb, sp * cb, cp * sb
                    dst = pl.ds(pl.multiple_of(k * LANES + h * ROWS, ROWS), ROWS)
                    values = (cc + ss, sc - cs, cc - ss, sc + cs, c0, c1, c2, c3, s0, s1_, s2_, s3)
                    for n, v in enumerate(values):
                        state[n, dst, :] = v.astype(BF16)
                return 0

            lax.fori_loop(start, stop, panel, 0)

        setup1 = functools.partial(setup, state1, air_ref, column1, 3.0)
        setup2 = functools.partial(setup, state2, obs_ref, column2, 4.0)
        columns(column1, src_ref)
        columns(column2, air_ref)

        setup1(0, CUT[0])
        pl.semaphore_wait(barrier, len(peers))

        x_sends = [
            send(part.at[(x + d) % 4], recv_x.at[d - 1], sx.at[d - 1], rx.at[d - 1], x_peer(d)) for d in (2, 1, 3)
        ]
        for s in x_sends:
            s.start()

        setup1(CUT[0], 32)
        setup2(0, CUT[1])

        for s in x_sends:
            s.wait_recv()
        row = lax.broadcasted_iota(jnp.int32, (64, LANES), 0)
        even = row % 2 == 0
        total = part[x] + recv_x[0] + recv_x[1] + recv_x[2]
        quarter = ((row_freq(row) + 1) * blade_ref[...]) & 3
        cos_q = (quarter == 0).astype(F32) - (quarter == 2).astype(F32)
        sin_q = (quarter == 1).astype(F32) - (quarter == 3).astype(F32)
        turned = total * cos_q + swapped(total, even) * jnp.where(even, sin_q, -sin_q)
        own[...] = turned.reshape(2, 32, LANES)
        z_sends = [
            send(own.at[z_of(d) // 4], recv_z.at[z], sz.at[d - 1], rz.at[d - 1], z_peer(d))
            for d in (4, 3, 5, 2, 6, 1, 7)
        ]
        for s in z_sends:
            s.start()
        recv_z[z] = own[zh]

        setup2(CUT[1], CUT[2])

        def radiate(line, state, mine, recv, ssem, rsem, near):
            row = lax.broadcasted_iota(jnp.int32, (32, LANES), 0)
            even = row % 2 == 0
            side = jnp.where((row // 2) % 2 == 0, 1.0, -1.0).astype(F32)
            for zz in range(4):
                v = line(zz)
                hi = v.astype(BF16).astype(F32)
                kinds = []
                for piece in (hi, v - hi):
                    sw = swapped(piece, even)
                    sw = jnp.where(even, sw, -sw)
                    kinds.append((piece, piece * -side, sw, sw * side))
                for kind in range(4):
                    for jj in range(4):
                        pair = jnp.concatenate([q[kind][8 * jj : 8 * jj + 8] for q in kinds], axis=0)
                        lane = kind * 256 + (zz % 2) * LANES
                        weights[zz // 2, jj, :, lane : lane + LANES] = pair.astype(BF16)
            low = lax.broadcasted_iota(jnp.int32, (8, LANES), 0) < 4

            def copy(i):
                return send(mine.at[i], recv.at[i], ssem.at[i], rsem.at[i], (fi, block_panel(i)))

            def block(i, _):
                acc = [jnp.zeros((16, 256), F32)] * 4
                near_acc = jnp.zeros((64, LANES), F32)
                for kt in range(2):
                    rows = pl.ds(pl.multiple_of(i * 512 + kt * 256, 256), 256)
                    ec0, es0, ec1, es1 = (state[n, rows, :] for n in range(4))
                    for jj in range(4):
                        cj, sj = state[4 + jj, rows, :], state[8 + jj, rows, :]
                        big = jnp.concatenate(
                            [
                                jnp.concatenate([ec0 * cj, ec1 * cj], axis=1),
                                jnp.concatenate([es0 * sj, es1 * sj], axis=1),
                                jnp.concatenate([es0 * cj, es1 * cj], axis=1),
                                jnp.concatenate([ec0 * sj, ec1 * sj], axis=1),
                            ],
                            axis=0,
                        )
                        acc[jj] = acc[jj] + jnp.dot(weights[kt, jj], big, preferred_element_type=F32)
                    if near:
                        left = jnp.concatenate([weights[kt, jj, :, 0:256] for jj in range(4)], axis=0)
                        near_acc = near_acc + jnp.dot(left, hits[rows, :], preferred_element_type=F32)
                for jj in range(4):
                    both = acc[jj][0:8] + acc[jj][8:16]
                    out = jnp.where(low, both[:, :LANES], both[:, LANES:])
                    if near:
                        out = out + near_acc[16 * jj : 16 * jj + 8] + near_acc[16 * jj + 8 : 16 * jj + 16]
                    mine[i, 8 * jj : 8 * jj + 8, :] = out

                @pl.when(i < 7)
                def _():
                    copy(i).start()

                return 0

            lax.fori_loop(0, 8, block, 0)
            copies = [copy(i) for i in range(7)]
            total = mine[7]
            for i in range(7):
                copies[i].wait_recv()
                total = total + recv[i]
            return total, copies

        for s in z_sends:
            s.wait_recv()
        incident, sends1 = radiate(lambda zz: recv_z[zz] + recv_z[zz + 4], state1, mine1, recv1, s1, r1, False)
        line2[zl] = incident * reflect_ref[...]
        l_sends = [
            send(line2.at[zl], line2.at[zl], sl.at[d - 1], rl.at[d - 1], line_peer(d)) for d in (2, 1, 3)
        ]
        for s in l_sends:
            s.start()

        setup2(CUT[2], 32)

        def count(k, _):
            at = pl.multiple_of(block_panel(k // 4) * LANES, LANES)
            first = ((k % 4) * 8 + y * 2 + c) * LANES
            index = lax.broadcasted_iota(jnp.int32, (LANES, LANES), 0)
            total = jnp.zeros((LANES, LANES), F32)
            for n in range(4):
                total = total + jnp.where(index == near_ref[n : n + 1, pl.ds(at, LANES)] - first, 0.5, 0.0)
            hits[pl.ds(pl.multiple_of(k * LANES, LANES), LANES), :] = total.astype(BF16)
            return 0

        lax.fori_loop(0, PANELS, count, 0)

        for s in l_sends:
            s.wait_recv()
        observed, sends2 = radiate(lambda zz: line2[zz], state2, mine2, recv2, s2, r2, True)
        spec[fi] = observed

        f_sends = [send(spec.at[fi], spec.at[fi], sf.at[0], rf.at[0], half_peer)]
        f_sends += [send(spec.at[fi], spec.at[fi], sf.at[d], rf.at[d], x_peer(d)) for d in (2, 1, 3)]
        other = x * 2 + (1 - zh)
        f_sends += [send(spec.at[other], spec.at[other], sf.at[3 + d], rf.at[3 + d], x_peer(d)) for d in (2, 1, 3)]
        for s in f_sends[:4]:
            s.start()

        def back_rows(i, _):
            col = lax.broadcasted_iota(jnp.int32, (32, 256), 1)
            t = lax.broadcasted_iota(jnp.int32, (32, 256), 0) + fi * T_DEV + i * 32
            m = (col // 32) * F_DEV + row_freq(col) + 1
            value = turn_cos(m * t + 1024 * (col % 2))
            hi = value.astype(BF16)
            dst = pl.ds(pl.multiple_of(i * 32, 32), 32)
            back_hi[dst, :] = hi
            back_lo[dst, :] = (value - hi.astype(F32)).astype(BF16)
            return 0

        lax.fori_loop(0, T_DEV // 32, back_rows, 0)
        f_sends[0].wait_recv()
        for s in f_sends[4:]:
            s.start()
        for s in f_sends[1:]:
            s.wait_recv()

        seen = spec[...].reshape(256, LANES) * (1.0 / 16.0)
        hi = seen.astype(BF16)
        lo = (seen - hi.astype(F32)).astype(BF16)
        wide = jnp.dot(back_hi[...], jnp.concatenate([hi, lo], axis=1), preferred_element_type=F32)
        narrow = jnp.dot(back_lo[...], hi, preferred_element_type=F32)
        out_ref[...] = wide[:, :LANES] + wide[:, LANES:] + narrow

        for s in x_sends + z_sends + sends1 + l_sends + sends2 + f_sends:
            s.wait_send()

    pl.run_scoped(
        work,
        pltpu.VMEM((256, T_DEV), BF16),
        pltpu.VMEM((12, 4096, LANES), BF16),
        pltpu.VMEM((12, 4096, LANES), BF16),
        pltpu.VMEM((4096, LANES), BF16),
        pltpu.VMEM((T_DEV, 256), BF16),
        pltpu.VMEM((T_DEV, 256), BF16),
        pltpu.VMEM((4, 3, LANES, LANES), F32),
        pltpu.VMEM((4, 3, LANES, LANES), F32),
        pltpu.VMEM((2, 4, 16, 1024), BF16),
    )


def on_device(load, blade, source, airframe, reflect, observer, near):
    vmem = pl.BlockSpec(memory_space=pltpu.VMEM)
    dma = pltpu.SemaphoreType.DMA
    slots = [(4, 64), (3, 64), (2, 32), (8, 32), (8, 32), (7, 32), (4, 32), (8, 32), (7, 32), (8, 32)]
    scratch = [pltpu.VMEM((*slot, LANES), F32) for slot in slots]
    scratch += [dma((n,)) for n in (3, 3, 7, 7, 7, 7, 3, 3, 7, 7, 7, 7)]
    return pl.pallas_call(
        body,
        out_shape=jax.ShapeDtypeStruct((T_DEV, LANES), F32),
        in_specs=[vmem] * 7,
        out_specs=vmem,
        scratch_shapes=scratch,
        compiler_params=pltpu.CompilerParams(
            collective_id=0, has_side_effects=True, vmem_limit_bytes=56 * 1024 * 1024
        ),
        name="rotor",
    )(load, blade.reshape(1, LANES), source, airframe, reflect.reshape(1, LANES), observer, near.T)


def solution(mesh):
    return jax.shard_map(
        on_device,
        mesh=mesh,
        in_specs=(P("freq", "panel"), P("panel"), P(), P(), P("panel"), P(), P()),
        out_specs=P("freq", "panel"),
        check_vma=False,
    )
```

```python
import functools
import math

import jax
import jax.numpy as jnp
import numpy as np
from jax import lax
from jax.experimental import pallas as pl
from jax.experimental.pallas import tpu as pltpu
from jax.sharding import PartitionSpec as P

MESH = pl.DeviceIdType.MESH
F32, BF16 = jnp.float32, jnp.bfloat16
TIMES = 4096
PANELS = 32
LANES = 128
T_DEV = 512
F_DEV = 16
CUT = (4, 1, 5)
ROWS = 64


def fitted(fn, low, high, degree):
    cheb = np.polynomial.chebyshev.Chebyshev.interpolate(fn, degree, [low, high])
    return [float(v) for v in cheb.convert(kind=np.polynomial.Polynomial).coef]


COS_TURN = fitted(lambda u: np.cos(2 * np.pi * np.sqrt(u)), 1e-12, 0.25, 6)
COS_HALF = fitted(lambda u: 2 * np.cos(0.075 * np.sqrt(u)), 0.99, 44.1, 3)
SIN_HALF = fitted(lambda u: 2 * np.sin(0.075 * np.sqrt(u)) / np.sqrt(u), 0.99, 44.1, 2)
BASE = 1.0 / (4.0 * np.pi * 8.0)
COS_BASE = fitted(lambda u: BASE * np.cos(2 * np.pi * np.sqrt(u)), 1e-12, 0.25, 5)
SIN_BASE = fitted(lambda u: BASE * np.sin(2 * np.pi * np.sqrt(u)) / np.sqrt(u), 1e-12, 0.25, 5)


def poly(coef, u):
    total = coef[-1] * u + coef[-2]
    for c in coef[-3::-1]:
        total = total * u + c
    return total


def row_freq(row):
    offset, base, side = (row // 8) % 4, (row // 4) % 2, (row // 2) % 2
    return 8 * base + jnp.where(side == 0, 4 + offset, 3 - offset)


def turn_cos(numbers):
    turn = (((numbers + 2048) & 4095) - 2048).astype(F32) * (1.0 / 4096.0)
    return poly(COS_TURN, turn * turn)


def swapped(v, even):
    n = v.shape[0]
    return jnp.where(even, pltpu.roll(v, n - 1, 0), pltpu.roll(v, 1, 0))


def body(
    load_in, blade_in, src_in, air_in, reflect_in, obs_in, near_in, out_ref,
    load_ref, blade_ref, src_ref, air_ref, reflect_ref, obs_ref, near_ref, s_in,
    part, recv_x, own, recv_z, mine1, recv1, line2, mine2, recv2, spec,
    sx, rx, sz, rz, s1, r1, sl, rl, s2, r2, sf, rf,
):
    fi, pi = lax.axis_index("freq"), lax.axis_index("panel")
    x, zh = fi // 2, fi % 2
    zl, y, c = pi // 8, (pi // 2) % 4, pi % 2
    z = zh * 4 + zl

    def x_peer(d):
        return (((x + d) % 4) * 2 + zh, pi)

    def z_of(d):
        return (z + d) % 8

    def z_peer(d):
        zz = (z + d) % 8
        return (x * 2 + zz // 4, (zz % 4) * 8 + y * 2 + c)

    def line_peer(d):
        return (fi, ((zl + d) % 4) * 8 + y * 2 + c)

    def block_panel(i):
        q = i // 2
        dy = (2 + q + q // 2 + 2 * (q // 3)) % 4
        return zl * 8 + ((y + dy) % 4) * 2 + (c + 1 - i % 2) % 2

    def send(src, dst, ssem, rsem, to):
        return pltpu.make_async_remote_copy(
            src_ref=src, dst_ref=dst, send_sem=ssem, recv_sem=rsem, device_id=to, device_id_type=MESH
        )

    outside = (load_in, src_in, air_in, obs_in, near_in, blade_in, reflect_in)
    inside = (load_ref, src_ref, air_ref, obs_ref, near_ref, blade_ref, reflect_ref)
    fetches = [pltpu.make_async_copy(a, b, s_in.at[n]) for n, (a, b) in enumerate(zip(outside, inside))]
    for fetch in fetches:
        fetch.start()
    barrier = pltpu.get_barrier_semaphore()
    peers = [x_peer(d) for d in (1, 2, 3)] + [z_peer(d) for d in range(1, 8)]
    peers += [(fi, block_panel(i)) for i in range(7)]
    for to in peers:
        pl.semaphore_signal(barrier, inc=1, device_id=to, device_id_type=MESH)

    def work(table, state1, state2, hits, back_hi, back_lo, column1, column2, weights):
        def table_rows(i, _):
            row = lax.broadcasted_iota(jnp.int32, (32, T_DEV), 0)
            t = lax.broadcasted_iota(jnp.int32, (32, T_DEV), 1) + fi * T_DEV
            m = i * F_DEV + row_freq(row) + 1
            table[pl.ds(pl.multiple_of(i * 32, 32), 32), :] = turn_cos(m * t + 1024 * (row % 2)).astype(BF16)
            return 0

        lax.fori_loop(0, 8, table_rows, 0)
        for fetch in fetches:
            fetch.wait()
        spectrum = jnp.dot(table[...], load_ref[...], preferred_element_type=F32) * (1.0 / 64.0)
        part[...] = spectrum.reshape(4, 64, LANES)

        def columns(column, anchors):
            def one(zz, _):
                lane = pl.multiple_of((zz * 8 + y * 2 + c) * LANES, LANES)
                for i in range(3):
                    row = jnp.broadcast_to(anchors[i : i + 1, pl.ds(lane, LANES)], (LANES, LANES))
                    column[zz, i] = row.T
                return 0

            lax.fori_loop(0, 4, one, 0)

        wave = (8.0 + 0.15 * (F_DEV * fi.astype(F32) + 7.5)) * (1.0 / (2.0 * math.pi))

        def setup(state, targets, column, lift, start, stop):
            def block(i, _):
                at = pl.multiple_of(block_panel(i) * LANES, LANES)
                tx, ty, tz = (targets[n : n + 1, pl.ds(at, LANES)] for n in range(3))
                tz = tz - lift
                for h in range(512 // ROWS):
                    zz, rows = h * ROWS // LANES, pl.ds(h * ROWS % LANES, ROWS)
                    dx, dy, dz = tx - column[zz, 0, rows, :], ty - column[zz, 1, rows, :], tz - column[zz, 2, rows, :]
                    square = dx * dx + dy * dy + dz * dz
                    inverse = lax.rsqrt(square)
                    r = square * inverse
                    turns = r * wave
                    turns = turns - jnp.round(turns)
                    u = turns * turns
                    cp = poly(COS_BASE, u) * inverse
                    sp = poly(SIN_BASE, u) * (turns * inverse)
                    c0 = poly(COS_HALF, square)
                    s0 = poly(SIN_HALF, square) * r
                    twice = c0 * c0 - 2.0
                    c1, s1_ = (twice - 1.0) * c0, (twice + 1.0) * s0
                    c2, s2_ = twice * c1 - c0, twice * s1_ - s0
                    c3, s3 = twice * c2 - c1, twice * s2_ - s1_
                    cb, sb = c3 * c0 - s3 * s0, s3 * c0 + c3 * s0
                    cp, sp, cb, sb = (v.astype(BF16) for v in (cp, sp, cb, sb))
                    cc, ss, sc, cs = cp * cb, sp * sb, sp * cb, cp * sb
                    dst = pl.ds(pl.multiple_of(i * 512 + h * ROWS, ROWS), ROWS)
                    values = (cc + ss, sc - cs, cc - ss, sc + cs, c0, c1, c2, c3, s0, s1_, s2_, s3)
                    for n, v in enumerate(values):
                        state[n, dst, :] = v.astype(BF16)
                return 0

            lax.fori_loop(start, stop, block, 0)

        setup1 = functools.partial(setup, state1, air_ref, column1, 3.0)
        setup2 = functools.partial(setup, state2, obs_ref, column2, 4.0)
        columns(column1, src_ref)
        columns(column2, air_ref)

        setup1(0, CUT[0])
        pl.semaphore_wait(barrier, len(peers))

        x_sends = [
            send(part.at[(x + d) % 4], recv_x.at[d - 1], sx.at[d - 1], rx.at[d - 1], x_peer(d)) for d in (2, 1, 3)
        ]
        for s in x_sends:
            s.start()

        setup1(CUT[0], 8)
        setup2(0, CUT[1])

        for s in x_sends:
            s.wait_recv()
        row = lax.broadcasted_iota(jnp.int32, (64, LANES), 0)
        even = row % 2 == 0
        total = part[x] + recv_x[0] + recv_x[1] + recv_x[2]
        quarter = ((row_freq(row) + 1) * blade_ref[...]) & 3
        cos_q = (quarter == 0).astype(F32) - (quarter == 2).astype(F32)
        sin_q = (quarter == 1).astype(F32) - (quarter == 3).astype(F32)
        turned = total * cos_q + swapped(total, even) * jnp.where(even, sin_q, -sin_q)
        own[...] = turned.reshape(2, 32, LANES)
        z_sends = [
            send(own.at[z_of(d) // 4], recv_z.at[z], sz.at[d - 1], rz.at[d - 1], z_peer(d))
            for d in (4, 3, 5, 2, 6, 1, 7)
        ]
        for s in z_sends:
            s.start()
        recv_z[z] = own[zh]

        setup2(CUT[1], CUT[2])

        def radiate(line, state, mine, recv, ssem, rsem, near):
            row = lax.broadcasted_iota(jnp.int32, (32, LANES), 0)
            even = row % 2 == 0
            side = jnp.where((row // 2) % 2 == 0, 1.0, -1.0).astype(F32)
            for zz in range(4):
                v = line(zz)
                hi = v.astype(BF16).astype(F32)
                kinds = []
                for piece in (hi, v - hi):
                    sw = swapped(piece, even)
                    sw = jnp.where(even, sw, -sw)
                    kinds.append((piece, piece * -side, sw, sw * side))
                for kind in range(4):
                    for jj in range(4):
                        pair = jnp.concatenate([q[kind][8 * jj : 8 * jj + 8] for q in kinds], axis=0)
                        lane = kind * 256 + (zz % 2) * LANES
                        weights[zz // 2, jj, :, lane : lane + LANES] = pair.astype(BF16)
            low = lax.broadcasted_iota(jnp.int32, (8, LANES), 0) < 4

            def copy(i):
                return send(mine.at[i], recv.at[i], ssem.at[i], rsem.at[i], (fi, block_panel(i)))

            def block(i, _):
                acc = [jnp.zeros((16, 256), F32)] * 4
                near_acc = jnp.zeros((64, LANES), F32)
                for kt in range(2):
                    rows = pl.ds(pl.multiple_of(i * 512 + kt * 256, 256), 256)
                    ec0, es0, ec1, es1 = (state[n, rows, :] for n in range(4))
                    for jj in range(4):
                        cj, sj = state[4 + jj, rows, :], state[8 + jj, rows, :]
                        big = jnp.concatenate(
                            [
                                jnp.concatenate([ec0 * cj, ec1 * cj], axis=1),
                                jnp.concatenate([es0 * sj, es1 * sj], axis=1),
                                jnp.concatenate([es0 * cj, es1 * cj], axis=1),
                                jnp.concatenate([ec0 * sj, ec1 * sj], axis=1),
                            ],
                            axis=0,
                        )
                        acc[jj] = acc[jj] + jnp.dot(weights[kt, jj], big, preferred_element_type=F32)
                    if near:
                        left = jnp.concatenate([weights[kt, jj, :, 0:256] for jj in range(4)], axis=0)
                        near_acc = near_acc + jnp.dot(left, hits[rows, :], preferred_element_type=F32)
                for jj in range(4):
                    both = acc[jj][0:8] + acc[jj][8:16]
                    out = jnp.where(low, both[:, :LANES], both[:, LANES:])
                    if near:
                        out = out + near_acc[16 * jj : 16 * jj + 8] + near_acc[16 * jj + 8 : 16 * jj + 16]
                    mine[i, 8 * jj : 8 * jj + 8, :] = out

                @pl.when(i < 7)
                def _():
                    copy(i).start()

                return 0

            lax.fori_loop(0, 8, block, 0)
            copies = [copy(i) for i in range(7)]
            total = mine[7]
            for i in range(7):
                copies[i].wait_recv()
                total = total + recv[i]
            return total, copies

        for s in z_sends:
            s.wait_recv()
        incident, sends1 = radiate(lambda zz: recv_z[zz] + recv_z[zz + 4], state1, mine1, recv1, s1, r1, False)
        line2[zl] = incident * reflect_ref[...]
        l_sends = [
            send(line2.at[zl], line2.at[zl], sl.at[d - 1], rl.at[d - 1], line_peer(d)) for d in (2, 1, 3)
        ]
        for s in l_sends:
            s.start()

        setup2(CUT[2], 8)

        def count(i, _):
            at = pl.multiple_of(block_panel(i) * LANES, LANES)
            near = [near_ref[n : n + 1, pl.ds(at, LANES)] - (y * 2 + c) * LANES for n in range(4)]
            for zz in range(4):
                index = lax.broadcasted_iota(jnp.int32, (LANES, LANES), 0) + zz * 8 * LANES
                total = jnp.where(index == near[0], 0.5, 0.0)
                for n in range(1, 4):
                    total = total + jnp.where(index == near[n], 0.5, 0.0)
                hits[pl.ds(pl.multiple_of(i * 512 + zz * LANES, LANES), LANES), :] = total.astype(BF16)
            return 0

        lax.fori_loop(0, 8, count, 0)

        for s in l_sends:
            s.wait_recv()
        observed, sends2 = radiate(lambda zz: line2[zz], state2, mine2, recv2, s2, r2, True)
        spec[fi] = observed

        f_sends = [
            send(spec.at[fi], spec.at[fi], sf.at[d - 1], rf.at[d - 1], ((fi + d) % 8, pi)) for d in range(1, 8)
        ]
        for s in f_sends:
            s.start()

        def back_rows(i, _):
            col = lax.broadcasted_iota(jnp.int32, (32, 256), 1)
            t = lax.broadcasted_iota(jnp.int32, (32, 256), 0) + fi * T_DEV + i * 32
            m = (col // 32) * F_DEV + row_freq(col) + 1
            value = turn_cos(m * t + 1024 * (col % 2))
            hi = value.astype(BF16)
            dst = pl.ds(pl.multiple_of(i * 32, 32), 32)
            back_hi[dst, :] = hi
            back_lo[dst, :] = (value - hi.astype(F32)).astype(BF16)
            return 0

        lax.fori_loop(0, T_DEV // 32, back_rows, 0)
        for s in f_sends:
            s.wait_recv()

        seen = spec[...].reshape(256, LANES) * (1.0 / 16.0)
        hi = seen.astype(BF16)
        lo = (seen - hi.astype(F32)).astype(BF16)
        wide = jnp.dot(back_hi[...], jnp.concatenate([hi, lo], axis=1), preferred_element_type=F32)
        narrow = jnp.dot(back_lo[...], hi, preferred_element_type=F32)
        out_ref[...] = wide[:, :LANES] + wide[:, LANES:] + narrow

        for s in x_sends + z_sends + sends1 + l_sends + sends2 + f_sends:
            s.wait_send()

    pl.run_scoped(
        work,
        pltpu.VMEM((256, T_DEV), BF16),
        pltpu.VMEM((12, 4096, LANES), BF16),
        pltpu.VMEM((12, 4096, LANES), BF16),
        pltpu.VMEM((4096, LANES), BF16),
        pltpu.VMEM((T_DEV, 256), BF16),
        pltpu.VMEM((T_DEV, 256), BF16),
        pltpu.VMEM((4, 3, LANES, LANES), F32),
        pltpu.VMEM((4, 3, LANES, LANES), F32),
        pltpu.VMEM((2, 4, 16, 1024), BF16),
    )


def on_device(load, blade, source, airframe, reflect, observer, near):
    args = (load, blade.reshape(1, LANES), source, airframe, reflect.reshape(1, LANES), observer, near.T)
    vmem = pl.BlockSpec(memory_space=pltpu.VMEM)
    dma = pltpu.SemaphoreType.DMA
    slots = [(4, 64), (3, 64), (2, 32), (8, 32), (8, 32), (7, 32), (4, 32), (8, 32), (7, 32), (8, 32)]
    scratch = [pltpu.VMEM(a.shape, a.dtype) for a in args] + [dma((7,))]
    scratch += [pltpu.VMEM((*slot, LANES), F32) for slot in slots]
    scratch += [dma((n,)) for n in (3, 3, 7, 7, 7, 7, 3, 3, 7, 7, 7, 7)]
    return pl.pallas_call(
        body,
        out_shape=jax.ShapeDtypeStruct((T_DEV, LANES), F32),
        in_specs=[pl.BlockSpec(memory_space=pl.ANY)] * 7,
        out_specs=vmem,
        scratch_shapes=scratch,
        compiler_params=pltpu.CompilerParams(
            collective_id=0, has_side_effects=True, vmem_limit_bytes=56 * 1024 * 1024
        ),
        name="rotor",
    )(*args)


def solution(mesh):
    return jax.shard_map(
        on_device,
        mesh=mesh,
        in_specs=(P("freq", "panel"), P("panel"), P(), P(), P("panel"), P(), P()),
        out_specs=P("freq", "panel"),
        check_vma=False,
    )
```

```python
import functools
import math

import jax
import jax.numpy as jnp
import numpy as np
from jax import lax
from jax.experimental import pallas as pl
from jax.experimental.pallas import tpu as pltpu
from jax.sharding import PartitionSpec as P

MESH = pl.DeviceIdType.MESH
F32, BF16 = jnp.float32, jnp.bfloat16
TIMES = 4096
PANELS = 32
LANES = 128
T_DEV = 512
F_DEV = 16
CUT = (4, 2, 4)
ROWS = 32


def fitted(fn, low, high, degree):
    cheb = np.polynomial.chebyshev.Chebyshev.interpolate(fn, degree, [low, high])
    return [float(v) for v in cheb.convert(kind=np.polynomial.Polynomial).coef]


COS_TURN = fitted(lambda u: np.cos(2 * np.pi * np.sqrt(u)), 1e-12, 0.25, 6)
COS_HALF = fitted(lambda u: 2 * np.cos(0.075 * np.sqrt(u)), 0.99, 44.1, 3)
SIN_HALF = fitted(lambda u: 2 * np.sin(0.075 * np.sqrt(u)) / np.sqrt(u), 0.99, 44.1, 2)
BASE = 1.0 / (4.0 * np.pi * 8.0)
COS_BASE = fitted(lambda u: BASE * np.cos(2 * np.pi * np.sqrt(u)), 1e-12, 0.25, 5)
SIN_BASE = fitted(lambda u: BASE * np.sin(2 * np.pi * np.sqrt(u)) / np.sqrt(u), 1e-12, 0.25, 5)


def poly(coef, u):
    total = coef[-1] * u + coef[-2]
    for c in coef[-3::-1]:
        total = total * u + c
    return total


def row_freq(row):
    offset, base, side = (row // 8) % 4, (row // 4) % 2, (row // 2) % 2
    return 8 * base + jnp.where(side == 0, 4 + offset, 3 - offset)


def turn_cos(numbers):
    turn = (((numbers + 2048) & 4095) - 2048).astype(F32) * (1.0 / 4096.0)
    return poly(COS_TURN, turn * turn)


def swapped(v, even):
    n = v.shape[0]
    return jnp.where(even, pltpu.roll(v, n - 1, 0), pltpu.roll(v, 1, 0))


def body(
    load_in, blade_in, src_in, air_in, reflect_in, obs_in, near_in, seen_ref, back_hi, back_lo,
    load_ref, blade_ref, src_ref, air_ref, reflect_ref, obs_ref, near_ref, s_in, relay,
    part, recv_x, own, recv_z, mine1, recv1, line2, mine2, recv2, spec,
    sx, rx, sz, rz, s1, r1, sl, rl, s2, r2, sf, rf,
):
    fi, pi = lax.axis_index("freq"), lax.axis_index("panel")
    x, zh = fi // 2, fi % 2
    zl, y, c = pi // 8, (pi // 2) % 4, pi % 2
    z = zh * 4 + zl

    def x_peer(d):
        return (((x + d) % 4) * 2 + zh, pi)

    def z_of(d):
        return (z + d) % 8

    def z_peer(d):
        zz = (z + d) % 8
        return (x * 2 + zz // 4, (zz % 4) * 8 + y * 2 + c)

    def line_peer(d):
        return (fi, ((zl + d) % 4) * 8 + y * 2 + c)

    def block_panel(i):
        q = i // 2
        dy = (2 + q + q // 2 + 2 * (q // 3)) % 4
        return zl * 8 + ((y + dy) % 4) * 2 + (c + 1 - i % 2) % 2

    def send(src, dst, ssem, rsem, to):
        return pltpu.make_async_remote_copy(
            src_ref=src, dst_ref=dst, send_sem=ssem, recv_sem=rsem, device_id=to, device_id_type=MESH
        )

    outside = (load_in, src_in, air_in, obs_in, near_in, blade_in, reflect_in)
    inside = (load_ref, src_ref, air_ref, obs_ref, near_ref, blade_ref, reflect_ref)
    fetches = [pltpu.make_async_copy(a, b, s_in.at[n]) for n, (a, b) in enumerate(zip(outside, inside))]
    for fetch in fetches:
        fetch.start()
    barrier = pltpu.get_barrier_semaphore()
    peers = [x_peer(d) for d in (1, 2, 3)] + [z_peer(d) for d in (1, 2, 6, 7)]
    peers += [(fi, block_panel(i)) for i in range(7)]
    for to in peers:
        pl.semaphore_signal(barrier, inc=1, device_id=to, device_id_type=MESH)

    def work(table, state1, state2, hits, column1, column2, weights):
        def table_rows(i, _):
            row = lax.broadcasted_iota(jnp.int32, (32, T_DEV), 0)
            t = lax.broadcasted_iota(jnp.int32, (32, T_DEV), 1) + fi * T_DEV
            m = i * F_DEV + row_freq(row) + 1
            table[pl.ds(pl.multiple_of(i * 32, 32), 32), :] = turn_cos(m * t + 1024 * (row % 2)).astype(BF16)
            return 0

        lax.fori_loop(0, 8, table_rows, 0)
        for fetch in fetches:
            fetch.wait()
        spectrum = jnp.dot(table[...], load_ref[...], preferred_element_type=F32) * (1.0 / 64.0)
        part[...] = spectrum.reshape(4, 64, LANES)

        def columns(column, anchors):
            def one(zz, _):
                lane = pl.multiple_of((zz * 8 + y * 2 + c) * LANES, LANES)
                for i in range(3):
                    row = jnp.broadcast_to(anchors[i : i + 1, pl.ds(lane, LANES)], (LANES, LANES))
                    column[zz, i] = row.T
                return 0

            lax.fori_loop(0, 4, one, 0)

        wave = (8.0 + 0.15 * (F_DEV * fi.astype(F32) + 7.5)) * (1.0 / (2.0 * math.pi))

        def setup(state, targets, column, lift, start, stop):
            def block(i, _):
                at = pl.multiple_of(block_panel(i) * LANES, LANES)
                tx, ty, tz = (targets[n : n + 1, pl.ds(at, LANES)] for n in range(3))
                tz = tz - lift
                for h in range(512 // ROWS):
                    zz, rows = h * ROWS // LANES, pl.ds(h * ROWS % LANES, ROWS)
                    dx, dy, dz = tx - column[zz, 0, rows, :], ty - column[zz, 1, rows, :], tz - column[zz, 2, rows, :]
                    square = dx * dx + dy * dy + dz * dz
                    inverse = lax.rsqrt(square)
                    r = square * inverse
                    turns = r * wave
                    turns = turns - jnp.round(turns)
                    u = turns * turns
                    cp = poly(COS_BASE, u) * inverse
                    sp = poly(SIN_BASE, u) * (turns * inverse)
                    c0 = poly(COS_HALF, square)
                    s0 = poly(SIN_HALF, square) * r
                    twice = c0 * c0 - 2.0
                    c1, s1_ = (twice - 1.0) * c0, (twice + 1.0) * s0
                    c2, s2_ = twice * c1 - c0, twice * s1_ - s0
                    c3, s3 = twice * c2 - c1, twice * s2_ - s1_
                    cb, sb = c3 * c0 - s3 * s0, s3 * c0 + c3 * s0
                    cp, sp, cb, sb = (v.astype(BF16) for v in (cp, sp, cb, sb))
                    cc, ss, sc, cs = cp * cb, sp * sb, sp * cb, cp * sb
                    dst = pl.ds(pl.multiple_of(i * 512 + h * ROWS, ROWS), ROWS)
                    values = (cc + ss, sc - cs, cc - ss, sc + cs, c0, c1, c2, c3, s0, s1_, s2_, s3)
                    for n, v in enumerate(values):
                        state[n, dst, :] = v.astype(BF16)
                return 0

            lax.fori_loop(start, stop, block, 0)

        setup1 = functools.partial(setup, state1, air_ref, column1, 3.0)
        setup2 = functools.partial(setup, state2, obs_ref, column2, 4.0)
        pl.semaphore_wait(barrier, len(peers))

        x_sends = [
            send(part.at[(x + d) % 4], recv_x.at[d - 1], sx.at[d - 1], rx.at[d - 1], x_peer(d)) for d in (2, 1, 3)
        ]
        for s in x_sends:
            s.start()
        for d in (2, 6):
            pl.semaphore_signal(relay, inc=1, device_id=z_peer(d), device_id_type=MESH)

        columns(column1, src_ref)
        setup1(0, CUT[0])

        for s in x_sends:
            s.wait_recv()
        row = lax.broadcasted_iota(jnp.int32, (64, LANES), 0)
        even = row % 2 == 0
        total = part[x] + recv_x[0] + recv_x[1] + recv_x[2]
        quarter = ((row_freq(row) + 1) * blade_ref[...]) & 3
        cos_q = (quarter == 0).astype(F32) - (quarter == 2).astype(F32)
        sin_q = (quarter == 1).astype(F32) - (quarter == 3).astype(F32)
        turned = total * cos_q + swapped(total, even) * jnp.where(even, sin_q, -sin_q)
        own[...] = turned.reshape(2, 32, LANES)
        z_sends = [
            send(own.at[z_of(d) // 4], recv_z.at[z], sz.at[d - 1], rz.at[d - 1], z_peer(d))
            for d in (4, 3, 5, 2, 6, 1, 7)
        ]
        pl.semaphore_wait(relay, 2)
        for s in z_sends:
            s.start()
        recv_z[z] = own[zh]

        setup1(CUT[0], 8)
        columns(column2, air_ref)
        setup2(0, CUT[1])

        def radiate(line, state, mine, recv, ssem, rsem, near, beside):
            row = lax.broadcasted_iota(jnp.int32, (32, LANES), 0)
            even = row % 2 == 0
            side = jnp.where((row // 2) % 2 == 0, 1.0, -1.0).astype(F32)
            for zz in range(4):
                v = line(zz)
                hi = v.astype(BF16).astype(F32)
                kinds = []
                for piece in (hi, v - hi):
                    sw = swapped(piece, even)
                    sw = jnp.where(even, sw, -sw)
                    kinds.append((piece, piece * -side, sw, sw * side))
                for kind in range(4):
                    for jj in range(4):
                        pair = jnp.concatenate([q[kind][8 * jj : 8 * jj + 8] for q in kinds], axis=0)
                        lane = kind * 256 + (zz % 2) * LANES
                        weights[zz // 2, jj, :, lane : lane + LANES] = pair.astype(BF16)
            low = lax.broadcasted_iota(jnp.int32, (8, LANES), 0) < 4

            def copy(i):
                return send(mine.at[i], recv.at[i], ssem.at[i], rsem.at[i], (fi, block_panel(i)))

            def block(i, _):
                acc = [jnp.zeros((16, 256), F32)] * 4
                near_acc = jnp.zeros((64, LANES), F32)
                for kt in range(2):
                    rows = pl.ds(pl.multiple_of(i * 512 + kt * 256, 256), 256)
                    ec0, es0, ec1, es1 = (state[n, rows, :] for n in range(4))
                    for jj in range(4):
                        cj, sj = state[4 + jj, rows, :], state[8 + jj, rows, :]
                        big = jnp.concatenate(
                            [
                                jnp.concatenate([ec0 * cj, ec1 * cj], axis=1),
                                jnp.concatenate([es0 * sj, es1 * sj], axis=1),
                                jnp.concatenate([es0 * cj, es1 * cj], axis=1),
                                jnp.concatenate([ec0 * sj, ec1 * sj], axis=1),
                            ],
                            axis=0,
                        )
                        acc[jj] = acc[jj] + jnp.dot(weights[kt, jj], big, preferred_element_type=F32)
                    if near:
                        left = jnp.concatenate([weights[kt, jj, :, 0:256] for jj in range(4)], axis=0)
                        near_acc = near_acc + jnp.dot(left, hits[rows, :], preferred_element_type=F32)
                for jj in range(4):
                    both = acc[jj][0:8] + acc[jj][8:16]
                    out = jnp.where(low, both[:, :LANES], both[:, LANES:])
                    if near:
                        out = out + near_acc[16 * jj : 16 * jj + 8] + near_acc[16 * jj + 8 : 16 * jj + 16]
                    mine[i, 8 * jj : 8 * jj + 8, :] = out

                @pl.when(i < 7)
                def _():
                    copy(i).start()

                return 0

            lax.fori_loop(0, 8, block, 0)
            beside()
            copies = [copy(i) for i in range(7)]
            total = mine[7]
            for i in range(7):
                copies[i].wait_recv()
                total = total + recv[i]
            return total, copies

        def count(i, _):
            at = pl.multiple_of(block_panel(i) * LANES, LANES)
            near = [near_ref[n : n + 1, pl.ds(at, LANES)] - (y * 2 + c) * LANES for n in range(4)]
            for zz in range(4):
                index = lax.broadcasted_iota(jnp.int32, (LANES, LANES), 0) + zz * 8 * LANES
                total = jnp.where(index == near[0], 0.5, 0.0)
                for n in range(1, 4):
                    total = total + jnp.where(index == near[n], 0.5, 0.0)
                hits[pl.ds(pl.multiple_of(i * 512 + zz * LANES, LANES), LANES), :] = total.astype(BF16)
            return 0

        def tail1():
            lax.fori_loop(0, 8, count, 0)
            setup2(CUT[1], CUT[2])

        for s in z_sends:
            s.wait_recv()
        incident, sends1 = radiate(lambda zz: recv_z[zz] + recv_z[zz + 4], state1, mine1, recv1, s1, r1, False, tail1)
        line2[zl] = incident * reflect_ref[...]
        l_sends = [
            send(line2.at[zl], line2.at[zl], sl.at[d - 1], rl.at[d - 1], line_peer(d)) for d in (2, 1, 3)
        ]
        for s in l_sends:
            s.start()

        setup2(CUT[2], 8)


        for s in l_sends:
            s.wait_recv()
        observed, sends2 = radiate(lambda zz: line2[zz], state2, mine2, recv2, s2, r2, True, lambda: None)
        spec[fi] = observed

        f_sends = [
            send(spec.at[fi], spec.at[fi], sf.at[d - 1], rf.at[d - 1], ((fi + d) % 8, pi)) for d in range(1, 8)
        ]
        for s in f_sends:
            s.start()

        def back_rows(i, _):
            col = lax.broadcasted_iota(jnp.int32, (32, 256), 1)
            t = lax.broadcasted_iota(jnp.int32, (32, 256), 0) + fi * T_DEV + i * 32
            m = (col // 32) * F_DEV + row_freq(col) + 1
            value = turn_cos(m * t + 1024 * (col % 2))
            hi = value.astype(BF16)
            dst = pl.ds(pl.multiple_of(i * 32, 32), 32)
            back_hi[dst, :] = hi
            back_lo[dst, :] = (value - hi.astype(F32)).astype(BF16)
            return 0

        lax.fori_loop(0, T_DEV // 32, back_rows, 0)
        for s in f_sends:
            s.wait_recv()

        seen = spec[...].reshape(256, LANES) * (1.0 / 16.0)
        hi = seen.astype(BF16)
        lo = (seen - hi.astype(F32)).astype(BF16)
        seen_ref[...] = jnp.concatenate([hi, lo], axis=1)

        for s in x_sends + z_sends + sends1 + l_sends + sends2 + f_sends:
            s.wait_send()

    pl.run_scoped(
        work,
        pltpu.VMEM((256, T_DEV), BF16),
        pltpu.VMEM((12, 4096, LANES), BF16),
        pltpu.VMEM((12, 4096, LANES), BF16),
        pltpu.VMEM((4096, LANES), BF16),
        pltpu.VMEM((4, 3, LANES, LANES), F32),
        pltpu.VMEM((4, 3, LANES, LANES), F32),
        pltpu.VMEM((2, 4, 16, 1024), BF16),
    )


def back(seen_ref, hi_ref, lo_ref, out_ref):
    wide = jnp.dot(hi_ref[...], seen_ref[...], preferred_element_type=F32)
    narrow = jnp.dot(lo_ref[...], seen_ref[:, :LANES], preferred_element_type=F32)
    out_ref[...] = wide[:, :LANES] + wide[:, LANES:] + narrow


def on_device(load, blade, source, airframe, reflect, observer, near):
    args = (load, blade.reshape(1, LANES), source, airframe, reflect.reshape(1, LANES), observer, near.T)
    args = tuple(pltpu.with_memory_space_constraint(a, pltpu.HBM) for a in args)
    vmem = pl.BlockSpec(memory_space=pltpu.VMEM)
    dma = pltpu.SemaphoreType.DMA
    slots = [(4, 64), (3, 64), (2, 32), (8, 32), (8, 32), (7, 32), (4, 32), (8, 32), (7, 32), (8, 32)]
    scratch = [pltpu.VMEM(a.shape, a.dtype) for a in args] + [dma((7,)), pltpu.SemaphoreType.REGULAR]
    scratch += [pltpu.VMEM((*slot, LANES), F32) for slot in slots]
    scratch += [dma((n,)) for n in (3, 3, 7, 7, 7, 7, 3, 3, 7, 7, 7, 7)]
    shapes = ((256, 256), (T_DEV, 256), (T_DEV, 256))
    parts = pl.pallas_call(
        body,
        out_shape=[jax.ShapeDtypeStruct(s, BF16) for s in shapes],
        in_specs=[pl.BlockSpec(memory_space=pltpu.HBM)] * 7,
        out_specs=[vmem] * 3,
        scratch_shapes=scratch,
        compiler_params=pltpu.CompilerParams(
            collective_id=0, has_side_effects=True, vmem_limit_bytes=40 * 1024 * 1024
        ),
        name="rotor",
    )(*args)
    return pl.pallas_call(
        back,
        out_shape=jax.ShapeDtypeStruct((T_DEV, LANES), F32),
        in_specs=[vmem] * 3,
        out_specs=vmem,
        compiler_params=pltpu.CompilerParams(vmem_limit_bytes=4 * 1024 * 1024),
        name="back",
    )(*parts)


def solution(mesh):
    return jax.shard_map(
        on_device,
        mesh=mesh,
        in_specs=(P("freq", "panel"), P("panel"), P(), P(), P("panel"), P(), P()),
        out_specs=P("freq", "panel"),
        check_vma=False,
    )
```

```python
import functools
import math

import jax
import jax.numpy as jnp
import numpy as np
from jax import lax
from jax.experimental import pallas as pl
from jax.experimental.pallas import tpu as pltpu
from jax.sharding import PartitionSpec as P

MESH = pl.DeviceIdType.MESH
F32, BF16 = jnp.float32, jnp.bfloat16
TIMES = 4096
PANELS = 32
LANES = 128
T_DEV = 512
F_DEV = 16
CUT = (4, 2, 4)
ROWS = 32


def fitted(fn, low, high, degree):
    cheb = np.polynomial.chebyshev.Chebyshev.interpolate(fn, degree, [low, high])
    return [float(v) for v in cheb.convert(kind=np.polynomial.Polynomial).coef]


COS_TURN = fitted(lambda u: np.cos(2 * np.pi * np.sqrt(u)), 1e-12, 0.25, 5)
COS_HALF = fitted(lambda u: 2 * np.cos(0.075 * np.sqrt(u)), 0.99, 44.1, 2)
SIN_HALF = fitted(lambda u: 2 * np.sin(0.075 * np.sqrt(u)) / np.sqrt(u), 0.99, 44.1, 2)
BASE = 1.0 / (4.0 * np.pi * 8.0)
COS_BASE = fitted(lambda u: BASE * np.cos(2 * np.pi * np.sqrt(u)), 1e-12, 0.25, 5)
SIN_BASE = fitted(lambda u: BASE * np.sin(2 * np.pi * np.sqrt(u)) / np.sqrt(u), 1e-12, 0.25, 4)


def poly(coef, u):
    total = coef[-1] * u + coef[-2]
    for c in coef[-3::-1]:
        total = total * u + c
    return total


def row_freq(row):
    offset, base, side = (row // 8) % 4, (row // 4) % 2, (row // 2) % 2
    return 8 * base + jnp.where(side == 0, 4 + offset, 3 - offset)


def turn_cos(numbers):
    turn = (((numbers + 2048) & 4095) - 2048).astype(F32) * (1.0 / 4096.0)
    return poly(COS_TURN, turn * turn)


def swapped(v, even):
    n = v.shape[0]
    return jnp.where(even, pltpu.roll(v, n - 1, 0), pltpu.roll(v, 1, 0))


def body(
    load_in, blade_in, src_in, air_in, reflect_in, obs_in, near_in, seen_ref, back_hi, back_lo,
    load_ref, blade_ref, src_ref, air_ref, reflect_ref, obs_ref, near_ref, s_in, relay,
    part, recv_x, own, recv_z, mine1, recv1, line2, mine2, recv2, spec,
    sx, rx, sz, rz, s1, r1, sl, rl, s2, r2, sf, rf,
):
    fi, pi = lax.axis_index("freq"), lax.axis_index("panel")
    x, zh = fi // 2, fi % 2
    zl, y, c = pi // 8, (pi // 2) % 4, pi % 2
    z = zh * 4 + zl

    def x_peer(d):
        return (((x + d) % 4) * 2 + zh, pi)

    def z_of(d):
        return (z + d) % 8

    def z_peer(d):
        zz = (z + d) % 8
        return (x * 2 + zz // 4, (zz % 4) * 8 + y * 2 + c)

    def line_peer(d):
        return (fi, ((zl + d) % 4) * 8 + y * 2 + c)

    def block_panel(i):
        q = i // 2
        dy = (2 + q + q // 2 + 2 * (q // 3)) % 4
        return zl * 8 + ((y + dy) % 4) * 2 + (c + 1 - i % 2) % 2

    def send(src, dst, ssem, rsem, to):
        return pltpu.make_async_remote_copy(
            src_ref=src, dst_ref=dst, send_sem=ssem, recv_sem=rsem, device_id=to, device_id_type=MESH
        )

    outside = (load_in, src_in, air_in, obs_in, near_in, blade_in, reflect_in)
    inside = (load_ref, src_ref, air_ref, obs_ref, near_ref, blade_ref, reflect_ref)
    fetches = [pltpu.make_async_copy(a, b, s_in.at[n]) for n, (a, b) in enumerate(zip(outside, inside))]
    for fetch in fetches:
        fetch.start()
    barrier = pltpu.get_barrier_semaphore()
    peers = [x_peer(d) for d in (1, 2, 3)] + [z_peer(d) for d in (1, 2, 6, 7)]
    peers += [(fi, block_panel(i)) for i in range(7)]
    for to in peers:
        pl.semaphore_signal(barrier, inc=1, device_id=to, device_id_type=MESH)

    def work(table, state1, state2, hits, column1, column2, weights):
        def table_rows(i, _):
            row = lax.broadcasted_iota(jnp.int32, (32, T_DEV), 0)
            t = lax.broadcasted_iota(jnp.int32, (32, T_DEV), 1) + fi * T_DEV
            m = i * F_DEV + row_freq(row) + 1
            table[pl.ds(pl.multiple_of(i * 32, 32), 32), :] = turn_cos(m * t + 1024 * (row % 2)).astype(BF16)
            return 0

        lax.fori_loop(0, 8, table_rows, 0)
        for fetch in fetches:
            fetch.wait()
        spectrum = jnp.dot(table[...], load_ref[...], preferred_element_type=F32) * (1.0 / 64.0)
        part[...] = spectrum.reshape(4, 64, LANES)

        def columns(column, anchors):
            def one(zz, _):
                lane = pl.multiple_of((zz * 8 + y * 2 + c) * LANES, LANES)
                for i in range(3):
                    row = jnp.broadcast_to(anchors[i : i + 1, pl.ds(lane, LANES)], (LANES, LANES))
                    column[zz, i] = row.T
                return 0

            lax.fori_loop(0, 4, one, 0)

        wave = (8.0 + 0.15 * (F_DEV * fi.astype(F32) + 7.5)) * (1.0 / (2.0 * math.pi))

        def setup(state, targets, column, lift, start, stop):
            def block(i, _):
                at = pl.multiple_of(block_panel(i) * LANES, LANES)
                tx, ty, tz = (targets[n : n + 1, pl.ds(at, LANES)] for n in range(3))
                tz = tz - lift
                for h in range(512 // ROWS):
                    zz, rows = h * ROWS // LANES, pl.ds(h * ROWS % LANES, ROWS)
                    dx, dy, dz = tx - column[zz, 0, rows, :], ty - column[zz, 1, rows, :], tz - column[zz, 2, rows, :]
                    square = dx * dx + dy * dy + dz * dz
                    inverse = lax.rsqrt(square)
                    r = square * inverse
                    turns = r * wave
                    turns = turns - jnp.round(turns)
                    u = turns * turns
                    cp = poly(COS_BASE, u) * inverse
                    sp = poly(SIN_BASE, u) * (turns * inverse)
                    c0 = poly(COS_HALF, square)
                    s0 = poly(SIN_HALF, square) * r
                    twice = c0 * c0 - 2.0
                    c1, s1_ = (twice - 1.0) * c0, (twice + 1.0) * s0
                    c2, s2_ = twice * c1 - c0, twice * s1_ - s0
                    c3, s3 = twice * c2 - c1, twice * s2_ - s1_
                    cb, sb = c3 * c0 - s3 * s0, s3 * c0 + c3 * s0
                    cp, sp, cb, sb = (v.astype(BF16) for v in (cp, sp, cb, sb))
                    cc, ss, sc, cs = cp * cb, sp * sb, sp * cb, cp * sb
                    dst = pl.ds(pl.multiple_of(i * 512 + h * ROWS, ROWS), ROWS)
                    values = (cc + ss, sc - cs, cc - ss, sc + cs, c0, c1, c2, c3, s0, s1_, s2_, s3)
                    for n, v in enumerate(values):
                        state[n, dst, :] = v.astype(BF16)
                return 0

            lax.fori_loop(start, stop, block, 0)

        setup1 = functools.partial(setup, state1, air_ref, column1, 3.0)
        setup2 = functools.partial(setup, state2, obs_ref, column2, 4.0)
        pl.semaphore_wait(barrier, len(peers))

        x_sends = [
            send(part.at[(x + d) % 4], recv_x.at[d - 1], sx.at[d - 1], rx.at[d - 1], x_peer(d)) for d in (2, 1, 3)
        ]
        for s in x_sends:
            s.start()
        for d in (2, 6):
            pl.semaphore_signal(relay, inc=1, device_id=z_peer(d), device_id_type=MESH)

        columns(column1, src_ref)
        setup1(0, CUT[0])

        for s in x_sends:
            s.wait_recv()
        row = lax.broadcasted_iota(jnp.int32, (64, LANES), 0)
        even = row % 2 == 0
        total = part[x] + recv_x[0] + recv_x[1] + recv_x[2]
        quarter = ((row_freq(row) + 1) * blade_ref[...]) & 3
        cos_q = (quarter == 0).astype(F32) - (quarter == 2).astype(F32)
        sin_q = (quarter == 1).astype(F32) - (quarter == 3).astype(F32)
        turned = total * cos_q + swapped(total, even) * jnp.where(even, sin_q, -sin_q)
        own[...] = turned.reshape(2, 32, LANES)
        z_sends = [
            send(own.at[z_of(d) // 4], recv_z.at[z], sz.at[d - 1], rz.at[d - 1], z_peer(d))
            for d in (4, 3, 5, 2, 6, 1, 7)
        ]
        pl.semaphore_wait(relay, 2)
        for s in z_sends:
            s.start()
        recv_z[z] = own[zh]

        setup1(CUT[0], 8)
        columns(column2, air_ref)
        setup2(0, CUT[1])

        def radiate(line, state, mine, recv, ssem, rsem, near, beside):
            row = lax.broadcasted_iota(jnp.int32, (32, LANES), 0)
            even = row % 2 == 0
            side = jnp.where((row // 2) % 2 == 0, 1.0, -1.0).astype(F32)
            for zz in range(4):
                v = line(zz)
                hi = v.astype(BF16).astype(F32)
                kinds = []
                for piece in (hi, v - hi):
                    sw = swapped(piece, even)
                    sw = jnp.where(even, sw, -sw)
                    kinds.append((piece, piece * -side, sw, sw * side))
                for kind in range(4):
                    for jj in range(4):
                        pair = jnp.concatenate([q[kind][8 * jj : 8 * jj + 8] for q in kinds], axis=0)
                        lane = kind * 256 + (zz % 2) * LANES
                        weights[zz // 2, jj, :, lane : lane + LANES] = pair.astype(BF16)
            low = lax.broadcasted_iota(jnp.int32, (8, LANES), 0) < 4

            def copy(i):
                return send(mine.at[i], recv.at[i], ssem.at[i], rsem.at[i], (fi, block_panel(i)))

            def block(i, _):
                acc = [jnp.zeros((16, 256), F32)] * 4
                near_acc = jnp.zeros((64, LANES), F32)
                for kt in range(2):
                    rows = pl.ds(pl.multiple_of(i * 512 + kt * 256, 256), 256)
                    ec0, es0, ec1, es1 = (state[n, rows, :] for n in range(4))
                    for jj in range(4):
                        cj, sj = state[4 + jj, rows, :], state[8 + jj, rows, :]
                        big = jnp.concatenate(
                            [
                                jnp.concatenate([ec0 * cj, ec1 * cj], axis=1),
                                jnp.concatenate([es0 * sj, es1 * sj], axis=1),
                                jnp.concatenate([es0 * cj, es1 * cj], axis=1),
                                jnp.concatenate([ec0 * sj, ec1 * sj], axis=1),
                            ],
                            axis=0,
                        )
                        acc[jj] = acc[jj] + jnp.dot(weights[kt, jj], big, preferred_element_type=F32)
                    if near:
                        left = jnp.concatenate([weights[kt, jj, :, 0:256] for jj in range(4)], axis=0)
                        near_acc = near_acc + jnp.dot(left, hits[rows, :], preferred_element_type=F32)
                for jj in range(4):
                    both = acc[jj][0:8] + acc[jj][8:16]
                    out = jnp.where(low, both[:, :LANES], both[:, LANES:])
                    if near:
                        out = out + near_acc[16 * jj : 16 * jj + 8] + near_acc[16 * jj + 8 : 16 * jj + 16]
                    mine[i, 8 * jj : 8 * jj + 8, :] = out

                @pl.when(i < 7)
                def _():
                    copy(i).start()

                return 0

            lax.fori_loop(0, 8, block, 0)
            beside()
            copies = [copy(i) for i in range(7)]
            total = mine[7]
            for i in range(7):
                copies[i].wait_recv()
                total = total + recv[i]
            return total, copies

        def count(i, _):
            at = pl.multiple_of(block_panel(i) * LANES, LANES)
            near = [near_ref[n : n + 1, pl.ds(at, LANES)] - (y * 2 + c) * LANES for n in range(4)]
            index = lax.broadcasted_iota(jnp.int32, (LANES, LANES), 0).astype(F32).astype(BF16)
            half, none = jnp.asarray(0.5, BF16), jnp.asarray(0.0, BF16)
            for zz in range(4):
                total = None
                for n in range(4):
                    local = near[n] - zz * 8 * LANES
                    local = jnp.where((local >= 0) & (local < LANES), local, -1).astype(F32).astype(BF16)
                    found = jnp.where(index == local, half, none)
                    total = found if total is None else total + found
                hits[pl.ds(pl.multiple_of(i * 512 + zz * LANES, LANES), LANES), :] = total
            return 0

        def tail1():
            lax.fori_loop(0, 8, count, 0)
            setup2(CUT[1], CUT[2])

        for s in z_sends:
            s.wait_recv()
        incident, sends1 = radiate(lambda zz: recv_z[zz] + recv_z[zz + 4], state1, mine1, recv1, s1, r1, False, tail1)
        line2[zl] = incident * reflect_ref[...]
        l_sends = [
            send(line2.at[zl], line2.at[zl], sl.at[d - 1], rl.at[d - 1], line_peer(d)) for d in (2, 1, 3)
        ]
        for s in l_sends:
            s.start()

        setup2(CUT[2], 8)


        for s in l_sends:
            s.wait_recv()
        observed, sends2 = radiate(lambda zz: line2[zz], state2, mine2, recv2, s2, r2, True, lambda: None)
        spec[fi] = observed

        f_sends = [
            send(spec.at[fi], spec.at[fi], sf.at[d - 1], rf.at[d - 1], ((fi + d) % 8, pi)) for d in range(1, 8)
        ]
        for s in f_sends:
            s.start()

        def back_rows(i, _):
            col = lax.broadcasted_iota(jnp.int32, (32, 256), 1)
            t = lax.broadcasted_iota(jnp.int32, (32, 256), 0) + fi * T_DEV + i * 32
            m = (col // 32) * F_DEV + row_freq(col) + 1
            value = turn_cos(m * t + 1024 * (col % 2))
            hi = value.astype(BF16)
            dst = pl.ds(pl.multiple_of(i * 32, 32), 32)
            back_hi[dst, :] = hi
            back_lo[dst, :] = (value - hi.astype(F32)).astype(BF16)
            return 0

        lax.fori_loop(0, T_DEV // 32, back_rows, 0)
        for s in f_sends:
            s.wait_recv()

        seen = spec[...].reshape(256, LANES) * (1.0 / 16.0)
        hi = seen.astype(BF16)
        lo = (seen - hi.astype(F32)).astype(BF16)
        seen_ref[...] = jnp.concatenate([hi, lo], axis=1)

        for s in x_sends + z_sends + sends1 + l_sends + sends2 + f_sends:
            s.wait_send()

    pl.run_scoped(
        work,
        pltpu.VMEM((256, T_DEV), BF16),
        pltpu.VMEM((12, 4096, LANES), BF16),
        pltpu.VMEM((12, 4096, LANES), BF16),
        pltpu.VMEM((4096, LANES), BF16),
        pltpu.VMEM((4, 3, LANES, LANES), F32),
        pltpu.VMEM((4, 3, LANES, LANES), F32),
        pltpu.VMEM((2, 4, 16, 1024), BF16),
    )


def back(seen_ref, hi_ref, lo_ref, out_ref, made, done):
    copies = []
    for q in range(4):
        rows = pl.ds(q * LANES, LANES)
        wide = jnp.dot(hi_ref[rows, :], seen_ref[...], preferred_element_type=F32)
        narrow = jnp.dot(lo_ref[rows, :], seen_ref[:, :LANES], preferred_element_type=F32)
        made[rows, :] = wide[:, :LANES] + wide[:, LANES:] + narrow
        copies.append(pltpu.make_async_copy(made.at[rows], out_ref.at[rows], done.at[q]))
        copies[q].start()
    for copy in copies:
        copy.wait()


def on_device(load, blade, source, airframe, reflect, observer, near):
    args = (load, blade.reshape(1, LANES), source, airframe, reflect.reshape(1, LANES), observer, near.T)
    args = tuple(pltpu.with_memory_space_constraint(a, pltpu.HBM) for a in args)
    vmem = pl.BlockSpec(memory_space=pltpu.VMEM)
    dma = pltpu.SemaphoreType.DMA
    slots = [(4, 64), (3, 64), (2, 32), (8, 32), (8, 32), (7, 32), (4, 32), (8, 32), (7, 32), (8, 32)]
    scratch = [pltpu.VMEM(a.shape, a.dtype) for a in args] + [dma((7,)), pltpu.SemaphoreType.REGULAR]
    scratch += [pltpu.VMEM((*slot, LANES), F32) for slot in slots]
    scratch += [dma((n,)) for n in (3, 3, 7, 7, 7, 7, 3, 3, 7, 7, 7, 7)]
    shapes = ((256, 256), (T_DEV, 256), (T_DEV, 256))
    parts = pl.pallas_call(
        body,
        out_shape=[jax.ShapeDtypeStruct(s, BF16) for s in shapes],
        in_specs=[pl.BlockSpec(memory_space=pltpu.HBM)] * 7,
        out_specs=[vmem] * 3,
        scratch_shapes=scratch,
        compiler_params=pltpu.CompilerParams(
            collective_id=0, has_side_effects=True, vmem_limit_bytes=40 * 1024 * 1024
        ),
        name="rotor",
    )(*args)
    return pl.pallas_call(
        back,
        out_shape=jax.ShapeDtypeStruct((T_DEV, LANES), F32),
        in_specs=[vmem] * 3,
        out_specs=pl.BlockSpec(memory_space=pl.ANY),
        scratch_shapes=[pltpu.VMEM((T_DEV, LANES), F32), dma((4,))],
        compiler_params=pltpu.CompilerParams(vmem_limit_bytes=4 * 1024 * 1024),
        name="back",
    )(*parts)


def solution(mesh):
    return jax.shard_map(
        on_device,
        mesh=mesh,
        in_specs=(P("freq", "panel"), P("panel"), P(), P(), P("panel"), P(), P()),
        out_specs=P("freq", "panel"),
        check_vma=False,
    )
```

```python
import functools
import math

import jax
import jax.numpy as jnp
import numpy as np
from jax import lax
from jax.experimental import pallas as pl
from jax.experimental.pallas import tpu as pltpu
from jax.sharding import PartitionSpec as P

MESH = pl.DeviceIdType.MESH
F32, BF16 = jnp.float32, jnp.bfloat16
TIMES = 4096
PANELS = 32
LANES = 128
T_DEV = 512
F_DEV = 16
CUT = (4, 2, 3)
ROWS = 32


def fitted(fn, low, high, degree):
    cheb = np.polynomial.chebyshev.Chebyshev.interpolate(fn, degree, [low, high])
    return [float(v) for v in cheb.convert(kind=np.polynomial.Polynomial).coef]


COS_TURN = fitted(lambda u: np.cos(2 * np.pi * np.sqrt(u)), 1e-12, 0.25, 5)
COS_HALF = fitted(lambda u: 2 * np.cos(0.075 * np.sqrt(u)), 0.99, 44.1, 2)
SIN_HALF = fitted(lambda u: 2 * np.sin(0.075 * np.sqrt(u)) / np.sqrt(u), 0.99, 44.1, 2)
BASE = 1.0 / (4.0 * np.pi * 8.0)
COS_BASE = fitted(lambda u: BASE * np.cos(2 * np.pi * np.sqrt(u)), 1e-12, 0.25, 5)
SIN_BASE = fitted(lambda u: BASE * np.sin(2 * np.pi * np.sqrt(u)) / np.sqrt(u), 1e-12, 0.25, 4)


def poly(coef, u):
    total = coef[-1] * u + coef[-2]
    for c in coef[-3::-1]:
        total = total * u + c
    return total


def row_freq(row):
    offset, base, side = (row // 8) % 4, (row // 4) % 2, (row // 2) % 2
    return 8 * base + jnp.where(side == 0, 4 + offset, 3 - offset)


def turn_cos(numbers):
    turn = (((numbers + 2048) & 4095) - 2048).astype(F32) * (1.0 / 4096.0)
    return poly(COS_TURN, turn * turn)


def swapped(v, even):
    n = v.shape[0]
    return jnp.where(even, pltpu.roll(v, n - 1, 0), pltpu.roll(v, 1, 0))


def body(
    load_in, blade_in, src_in, air_in, reflect_in, obs_in, near_in, seen_ref, back_hi, back_lo,
    load_ref, blade_ref, src_ref, air_ref, reflect_ref, obs_ref, near_ref, s_in, relay,
    part, recv_x, own, recv_z, mine1, recv1, line2, mine2, recv2, spec,
    sx, rx, sz, rz, s1, r1, sl, rl, s2, r2, sf, rf,
):
    fi, pi = lax.axis_index("freq"), lax.axis_index("panel")
    x, zh = fi // 2, fi % 2
    zl, y, c = pi // 8, (pi // 2) % 4, pi % 2
    z = zh * 4 + zl

    def x_peer(d):
        return (((x + d) % 4) * 2 + zh, pi)

    def z_of(d):
        return (z + d) % 8

    def z_peer(d):
        zz = (z + d) % 8
        return (x * 2 + zz // 4, (zz % 4) * 8 + y * 2 + c)

    def line_peer(d):
        return (fi, ((zl + d) % 4) * 8 + y * 2 + c)

    def block_panel(i):
        q = i // 2
        dy = (2 + q + q // 2 + 2 * (q // 3)) % 4
        return zl * 8 + ((y + dy) % 4) * 2 + (c + 1 - i % 2) % 2

    def send(src, dst, ssem, rsem, to):
        return pltpu.make_async_remote_copy(
            src_ref=src, dst_ref=dst, send_sem=ssem, recv_sem=rsem, device_id=to, device_id_type=MESH
        )

    outside = (load_in, src_in, air_in, obs_in, near_in, blade_in, reflect_in)
    inside = (load_ref, src_ref, air_ref, obs_ref, near_ref, blade_ref, reflect_ref)
    fetches = [pltpu.make_async_copy(a, b, s_in.at[n]) for n, (a, b) in enumerate(zip(outside, inside))]
    for fetch in fetches:
        fetch.start()
    barrier = pltpu.get_barrier_semaphore()
    peers = [x_peer(d) for d in (1, 2, 3)] + [z_peer(d) for d in (1, 2, 6, 7)]
    peers += [(fi, block_panel(i)) for i in range(7)]
    for to in peers:
        pl.semaphore_signal(barrier, inc=1, device_id=to, device_id_type=MESH)

    def work(table, state1, state2, hits, column1, column2, weights):
        def table_rows(i, _):
            row = lax.broadcasted_iota(jnp.int32, (32, T_DEV), 0)
            t = lax.broadcasted_iota(jnp.int32, (32, T_DEV), 1) + fi * T_DEV
            m = i * F_DEV + row_freq(row) + 1
            table[pl.ds(pl.multiple_of(i * 32, 32), 32), :] = turn_cos(m * t + 1024 * (row % 2)).astype(BF16)
            return 0

        lax.fori_loop(0, 8, table_rows, 0)
        for fetch in fetches:
            fetch.wait()
        spectrum = jnp.dot(table[...], load_ref[...], preferred_element_type=F32) * (1.0 / 64.0)
        part[...] = spectrum.reshape(4, 64, LANES)

        def columns(column, anchors):
            def one(zz, _):
                lane = pl.multiple_of((zz * 8 + y * 2 + c) * LANES, LANES)
                for i in range(3):
                    row = jnp.broadcast_to(anchors[i : i + 1, pl.ds(lane, LANES)], (LANES, LANES))
                    column[zz, i] = row.T
                return 0

            lax.fori_loop(0, 4, one, 0)

        wave = (8.0 + 0.15 * (F_DEV * fi.astype(F32) + 7.5)) * (1.0 / (2.0 * math.pi))

        def setup(state, targets, column, lift, start, stop):
            def block(i, _):
                at = pl.multiple_of(block_panel(i) * LANES, LANES)
                tx, ty, tz = (targets[n : n + 1, pl.ds(at, LANES)] for n in range(3))
                tz = tz - lift
                for h in range(512 // ROWS):
                    zz, rows = h * ROWS // LANES, pl.ds(h * ROWS % LANES, ROWS)
                    dx, dy, dz = tx - column[zz, 0, rows, :], ty - column[zz, 1, rows, :], tz - column[zz, 2, rows, :]
                    square = dx * dx + dy * dy + dz * dz
                    inverse = lax.rsqrt(square)
                    r = square * inverse
                    turns = r * wave
                    turns = turns - jnp.round(turns)
                    u = turns * turns
                    cp = poly(COS_BASE, u) * inverse
                    sp = poly(SIN_BASE, u) * (turns * inverse)
                    c0 = poly(COS_HALF, square)
                    s0 = poly(SIN_HALF, square) * r
                    twice = c0 * c0 - 2.0
                    c1, s1_ = (twice - 1.0) * c0, (twice + 1.0) * s0
                    c2, s2_ = twice * c1 - c0, twice * s1_ - s0
                    c3, s3 = twice * c2 - c1, twice * s2_ - s1_
                    cb, sb = c3 * c0 - s3 * s0, s3 * c0 + c3 * s0
                    cp, sp, cb, sb = (v.astype(BF16) for v in (cp, sp, cb, sb))
                    cc, ss, sc, cs = cp * cb, sp * sb, sp * cb, cp * sb
                    dst = pl.ds(pl.multiple_of(i * 512 + h * ROWS, ROWS), ROWS)
                    values = (cc + ss, sc - cs, cc - ss, sc + cs, c0, c1, c2, c3, s0, s1_, s2_, s3)
                    for n, v in enumerate(values):
                        state[n, dst, :] = v.astype(BF16)
                return 0

            lax.fori_loop(start, stop, block, 0)

        setup1 = functools.partial(setup, state1, air_ref, column1, 3.0)
        setup2 = functools.partial(setup, state2, obs_ref, column2, 4.0)
        pl.semaphore_wait(barrier, len(peers))

        x_sends = [
            send(part.at[(x + d) % 4], recv_x.at[d - 1], sx.at[d - 1], rx.at[d - 1], x_peer(d)) for d in (2, 1, 3)
        ]
        for s in x_sends:
            s.start()
        for d in (2, 6):
            pl.semaphore_signal(relay, inc=1, device_id=z_peer(d), device_id_type=MESH)

        columns(column1, src_ref)
        setup1(0, CUT[0])

        for s in x_sends:
            s.wait_recv()
        row = lax.broadcasted_iota(jnp.int32, (64, LANES), 0)
        even = row % 2 == 0
        total = part[x] + recv_x[0] + recv_x[1] + recv_x[2]
        quarter = ((row_freq(row) + 1) * blade_ref[...]) & 3
        cos_q = (quarter == 0).astype(F32) - (quarter == 2).astype(F32)
        sin_q = (quarter == 1).astype(F32) - (quarter == 3).astype(F32)
        turned = total * cos_q + swapped(total, even) * jnp.where(even, sin_q, -sin_q)
        own[...] = turned.reshape(2, 32, LANES)
        z_sends = [
            send(own.at[z_of(d) // 4], recv_z.at[z], sz.at[d - 1], rz.at[d - 1], z_peer(d))
            for d in (4, 3, 5, 2, 6, 1, 7)
        ]
        pl.semaphore_wait(relay, 2)
        for s in z_sends:
            s.start()
        recv_z[z] = own[zh]

        setup1(CUT[0], 8)
        columns(column2, air_ref)
        setup2(0, CUT[1])

        def radiate(line, state, mine, recv, ssem, rsem, near, beside):
            row = lax.broadcasted_iota(jnp.int32, (32, LANES), 0)
            even = row % 2 == 0
            side = jnp.where((row // 2) % 2 == 0, 1.0, -1.0).astype(F32)
            for zz in range(4):
                v = line(zz)
                hi = v.astype(BF16).astype(F32)
                kinds = []
                for piece in (hi, v - hi):
                    sw = swapped(piece, even)
                    sw = jnp.where(even, sw, -sw)
                    kinds.append((piece, piece * -side, sw, sw * side))
                for kind in range(4):
                    for jj in range(4):
                        pair = jnp.concatenate([q[kind][8 * jj : 8 * jj + 8] for q in kinds], axis=0)
                        lane = kind * 256 + (zz % 2) * LANES
                        weights[zz // 2, jj, :, lane : lane + LANES] = pair.astype(BF16)
            low = lax.broadcasted_iota(jnp.int32, (8, LANES), 0) < 4

            def copy(i):
                return send(mine.at[i], recv.at[i], ssem.at[i], rsem.at[i], (fi, block_panel(i)))

            def block(i, _):
                acc = [jnp.zeros((16, 256), F32)] * 4
                near_acc = jnp.zeros((64, LANES), F32)
                for kt in range(2):
                    rows = pl.ds(pl.multiple_of(i * 512 + kt * 256, 256), 256)
                    ec0, es0, ec1, es1 = (state[n, rows, :] for n in range(4))
                    for jj in range(4):
                        cj, sj = state[4 + jj, rows, :], state[8 + jj, rows, :]
                        big = jnp.concatenate(
                            [
                                jnp.concatenate([ec0 * cj, ec1 * cj], axis=1),
                                jnp.concatenate([es0 * sj, es1 * sj], axis=1),
                                jnp.concatenate([es0 * cj, es1 * cj], axis=1),
                                jnp.concatenate([ec0 * sj, ec1 * sj], axis=1),
                            ],
                            axis=0,
                        )
                        acc[jj] = acc[jj] + jnp.dot(weights[kt, jj], big, preferred_element_type=F32)
                    if near:
                        left = jnp.concatenate([weights[kt, jj, :, 0:256] for jj in range(4)], axis=0)
                        near_acc = near_acc + jnp.dot(left, hits[rows, :], preferred_element_type=F32)
                for jj in range(4):
                    both = acc[jj][0:8] + acc[jj][8:16]
                    out = jnp.where(low, both[:, :LANES], both[:, LANES:])
                    if near:
                        out = out + near_acc[16 * jj : 16 * jj + 8] + near_acc[16 * jj + 8 : 16 * jj + 16]
                    mine[i, 8 * jj : 8 * jj + 8, :] = out

                @pl.when(i < 7)
                def _():
                    copy(i).start()

                return 0

            lax.fori_loop(0, 8, block, 0)
            beside()
            copies = [copy(i) for i in range(7)]
            total = mine[7]
            for i in range(7):
                copies[i].wait_recv()
                total = total + recv[i]
            return total, copies

        def count(i, _):
            at = pl.multiple_of(block_panel(i) * LANES, LANES)
            near = [near_ref[n : n + 1, pl.ds(at, LANES)] - (y * 2 + c) * LANES for n in range(4)]
            index = lax.broadcasted_iota(jnp.int32, (LANES, LANES), 0).astype(F32).astype(BF16)
            half, none = jnp.asarray(0.5, BF16), jnp.asarray(0.0, BF16)
            for zz in range(4):
                total = None
                for n in range(4):
                    local = near[n] - zz * 8 * LANES
                    local = jnp.where((local >= 0) & (local < LANES), local, -1).astype(F32).astype(BF16)
                    found = jnp.where(index == local, half, none)
                    total = found if total is None else total + found
                hits[pl.ds(pl.multiple_of(i * 512 + zz * LANES, LANES), LANES), :] = total
            return 0

        def tail1():
            lax.fori_loop(0, 8, count, 0)
            setup2(CUT[1], CUT[2])

        for s in z_sends:
            s.wait_recv()
        incident, sends1 = radiate(lambda zz: recv_z[zz] + recv_z[zz + 4], state1, mine1, recv1, s1, r1, False, tail1)
        line2[zl] = incident * reflect_ref[...]
        l_sends = [
            send(line2.at[zl], line2.at[zl], sl.at[d - 1], rl.at[d - 1], line_peer(d)) for d in (2, 1, 3)
        ]
        for s in l_sends:
            s.start()

        setup2(CUT[2], 8)


        for s in l_sends:
            s.wait_recv()
        observed, sends2 = radiate(lambda zz: line2[zz], state2, mine2, recv2, s2, r2, True, lambda: None)
        spec[fi] = observed

        f_sends = [
            send(spec.at[fi], spec.at[fi], sf.at[d - 1], rf.at[d - 1], ((fi + d) % 8, pi)) for d in range(1, 8)
        ]
        for s in f_sends:
            s.start()

        def back_rows(i, _):
            col = lax.broadcasted_iota(jnp.int32, (32, 256), 1)
            t = lax.broadcasted_iota(jnp.int32, (32, 256), 0) + fi * T_DEV + i * 32
            m = (col // 32) * F_DEV + row_freq(col) + 1
            value = turn_cos(m * t + 1024 * (col % 2))
            hi = value.astype(BF16)
            dst = pl.ds(pl.multiple_of(i * 32, 32), 32)
            back_hi[dst, :] = hi
            back_lo[dst, :] = (value - hi.astype(F32)).astype(BF16)
            return 0

        lax.fori_loop(0, T_DEV // 32, back_rows, 0)
        for s in f_sends:
            s.wait_recv()

        seen = spec[...].reshape(256, LANES) * (1.0 / 16.0)
        hi = seen.astype(BF16)
        lo = (seen - hi.astype(F32)).astype(BF16)
        seen_ref[...] = jnp.concatenate([hi, lo], axis=1)

        for s in x_sends + z_sends + sends1 + l_sends + sends2 + f_sends:
            s.wait_send()

    pl.run_scoped(
        work,
        pltpu.VMEM((256, T_DEV), BF16),
        pltpu.VMEM((12, 4096, LANES), BF16),
        pltpu.VMEM((12, 4096, LANES), BF16),
        pltpu.VMEM((4096, LANES), BF16),
        pltpu.VMEM((4, 3, LANES, LANES), F32),
        pltpu.VMEM((4, 3, LANES, LANES), F32),
        pltpu.VMEM((2, 4, 16, 1024), BF16),
    )


def back(seen_ref, hi_ref, lo_ref, out_ref, made, done):
    copies = []
    for q in range(4):
        rows = pl.ds(q * LANES, LANES)
        wide = jnp.dot(hi_ref[rows, :], seen_ref[...], preferred_element_type=F32)
        narrow = jnp.dot(lo_ref[rows, :], seen_ref[:, :LANES], preferred_element_type=F32)
        made[rows, :] = wide[:, :LANES] + wide[:, LANES:] + narrow
        copies.append(pltpu.make_async_copy(made.at[rows], out_ref.at[rows], done.at[q]))
        copies[q].start()
    for copy in copies:
        copy.wait()


def on_device(load, blade, source, airframe, reflect, observer, near):
    args = (load, blade.reshape(1, LANES), source, airframe, reflect.reshape(1, LANES), observer, near.T)
    args = tuple(pltpu.with_memory_space_constraint(a, pltpu.HBM) for a in args)
    vmem = pl.BlockSpec(memory_space=pltpu.VMEM)
    dma = pltpu.SemaphoreType.DMA
    slots = [(4, 64), (3, 64), (2, 32), (8, 32), (8, 32), (7, 32), (4, 32), (8, 32), (7, 32), (8, 32)]
    scratch = [pltpu.VMEM(a.shape, a.dtype) for a in args] + [dma((7,)), pltpu.SemaphoreType.REGULAR]
    scratch += [pltpu.VMEM((*slot, LANES), F32) for slot in slots]
    scratch += [dma((n,)) for n in (3, 3, 7, 7, 7, 7, 3, 3, 7, 7, 7, 7)]
    shapes = ((256, 256), (T_DEV, 256), (T_DEV, 256))
    parts = pl.pallas_call(
        body,
        out_shape=[jax.ShapeDtypeStruct(s, BF16) for s in shapes],
        in_specs=[pl.BlockSpec(memory_space=pltpu.HBM)] * 7,
        out_specs=[vmem] * 3,
        scratch_shapes=scratch,
        compiler_params=pltpu.CompilerParams(
            collective_id=0, has_side_effects=True, vmem_limit_bytes=40 * 1024 * 1024
        ),
        name="rotor",
    )(*args)
    return pl.pallas_call(
        back,
        out_shape=jax.ShapeDtypeStruct((T_DEV, LANES), F32),
        in_specs=[vmem] * 3,
        out_specs=pl.BlockSpec(memory_space=pl.ANY),
        scratch_shapes=[pltpu.VMEM((T_DEV, LANES), F32), dma((4,))],
        compiler_params=pltpu.CompilerParams(vmem_limit_bytes=4 * 1024 * 1024),
        name="back",
    )(*parts)


def solution(mesh):
    return jax.shard_map(
        on_device,
        mesh=mesh,
        in_specs=(P("freq", "panel"), P("panel"), P(), P(), P("panel"), P(), P()),
        out_specs=P("freq", "panel"),
        check_vma=False,
    )
```

```python
import functools
import math

import jax
import jax.numpy as jnp
import numpy as np
from jax import lax
from jax.experimental import pallas as pl
from jax.experimental.pallas import tpu as pltpu
from jax.sharding import PartitionSpec as P

MESH = pl.DeviceIdType.MESH
F32, BF16 = jnp.float32, jnp.bfloat16
TIMES = 4096
PANELS = 32
LANES = 128
T_DEV = 512
F_DEV = 16
CUT = (4, 2, 3)
ROWS = 32


def fitted(fn, low, high, degree):
    cheb = np.polynomial.chebyshev.Chebyshev.interpolate(fn, degree, [low, high])
    return [float(v) for v in cheb.convert(kind=np.polynomial.Polynomial).coef]


COS_TURN = fitted(lambda u: np.cos(2 * np.pi * np.sqrt(u)), 1e-12, 0.25, 5)
COS_HALF = fitted(lambda u: 2 * np.cos(0.075 * np.sqrt(u)), 0.99, 44.1, 2)
SIN_HALF = fitted(lambda u: 2 * np.sin(0.075 * np.sqrt(u)) / np.sqrt(u), 0.99, 44.1, 2)
BASE = 1.0 / (4.0 * np.pi * 8.0)
COS_BASE = fitted(lambda u: BASE * np.cos(2 * np.pi * np.sqrt(u)), 1e-12, 0.25, 5)
SIN_BASE = fitted(lambda u: BASE * np.sin(2 * np.pi * np.sqrt(u)) / np.sqrt(u), 1e-12, 0.25, 4)


def poly(coef, u):
    total = coef[-1] * u + coef[-2]
    for c in coef[-3::-1]:
        total = total * u + c
    return total


def row_freq(row):
    offset, base, side = (row // 8) % 4, (row // 4) % 2, (row // 2) % 2
    return 8 * base + jnp.where(side == 0, 4 + offset, 3 - offset)


def turn_cos(numbers):
    turn = (((numbers + 2048) & 4095) - 2048).astype(F32) * (1.0 / 4096.0)
    return poly(COS_TURN, turn * turn)


def swapped(v, even):
    n = v.shape[0]
    return jnp.where(even, pltpu.roll(v, n - 1, 0), pltpu.roll(v, 1, 0))


def body(
    load_in, blade_in, src_in, air_in, reflect_in, obs_in, near_in, seen_ref, back_hi, back_lo,
    load_ref, blade_ref, src_ref, air_ref, reflect_ref, obs_ref, near_ref, s_in, relay,
    part, recv_x, own, recv_z, mine1, recv1, line2, mine2, recv2, spec,
    sx, rx, sz, rz, s1, r1, sl, rl, s2, r2, sf, rf,
):
    fi, pi = lax.axis_index("freq"), lax.axis_index("panel")
    x, zh = fi // 2, fi % 2
    zl, y, c = pi // 8, (pi // 2) % 4, pi % 2
    z = zh * 4 + zl

    def x_peer(d):
        return (((x + d) % 4) * 2 + zh, pi)

    def z_of(d):
        return (z + d) % 8

    def z_peer(d):
        zz = (z + d) % 8
        return (x * 2 + zz // 4, (zz % 4) * 8 + y * 2 + c)

    def line_peer(d):
        return (fi, ((zl + d) % 4) * 8 + y * 2 + c)

    def block_panel(i):
        q = i // 2
        dy = (2 + q + q // 2 + 2 * (q // 3)) % 4
        return zl * 8 + ((y + dy) % 4) * 2 + (c + 1 - i % 2) % 2

    def send(src, dst, ssem, rsem, to):
        return pltpu.make_async_remote_copy(
            src_ref=src, dst_ref=dst, send_sem=ssem, recv_sem=rsem, device_id=to, device_id_type=MESH
        )

    outside = (load_in, src_in, air_in, obs_in, near_in, blade_in, reflect_in)
    inside = (load_ref, src_ref, air_ref, obs_ref, near_ref, blade_ref, reflect_ref)
    fetches = [pltpu.make_async_copy(a, b, s_in.at[n]) for n, (a, b) in enumerate(zip(outside, inside))]
    fetches[0].start()
    barrier = pltpu.get_barrier_semaphore()
    peers = [x_peer(d) for d in (1, 2, 3)] + [z_peer(d) for d in (1, 2, 6, 7)]
    peers += [(fi, block_panel(i)) for i in range(7)]
    for to in peers:
        pl.semaphore_signal(barrier, inc=1, device_id=to, device_id_type=MESH)
    for fetch in fetches[1:]:
        fetch.start()

    def work(table, state1, state2, hits, column1, column2, weights):
        def table_rows(i, _):
            row = lax.broadcasted_iota(jnp.int32, (32, T_DEV), 0)
            t = lax.broadcasted_iota(jnp.int32, (32, T_DEV), 1) + fi * T_DEV
            m = i * F_DEV + row_freq(row) + 1
            table[pl.ds(pl.multiple_of(i * 32, 32), 32), :] = turn_cos(m * t + 1024 * (row % 2)).astype(BF16)
            return 0

        lax.fori_loop(0, 8, table_rows, 0)
        fetches[0].wait()
        spectrum = jnp.dot(table[...], load_ref[...], preferred_element_type=F32) * (1.0 / 64.0)
        part[...] = spectrum.reshape(4, 64, LANES)

        def columns(column, anchors):
            def one(zz, _):
                lane = pl.multiple_of((zz * 8 + y * 2 + c) * LANES, LANES)
                for i in range(3):
                    row = jnp.broadcast_to(anchors[i : i + 1, pl.ds(lane, LANES)], (LANES, LANES))
                    column[zz, i] = row.T
                return 0

            lax.fori_loop(0, 4, one, 0)

        wave = (8.0 + 0.15 * (F_DEV * fi.astype(F32) + 7.5)) * (1.0 / (2.0 * math.pi))

        def setup(state, targets, column, lift, start, stop):
            def block(i, _):
                at = pl.multiple_of(block_panel(i) * LANES, LANES)
                tx, ty, tz = (targets[n : n + 1, pl.ds(at, LANES)] for n in range(3))
                tz = tz - lift
                for h in range(512 // ROWS):
                    zz, rows = h * ROWS // LANES, pl.ds(h * ROWS % LANES, ROWS)
                    dx, dy, dz = tx - column[zz, 0, rows, :], ty - column[zz, 1, rows, :], tz - column[zz, 2, rows, :]
                    square = dx * dx + dy * dy + dz * dz
                    inverse = lax.rsqrt(square)
                    r = square * inverse
                    turns = r * wave
                    turns = turns - jnp.round(turns)
                    u = turns * turns
                    cp = poly(COS_BASE, u) * inverse
                    sp = poly(SIN_BASE, u) * (turns * inverse)
                    c0 = poly(COS_HALF, square)
                    s0 = poly(SIN_HALF, square) * r
                    twice = c0 * c0 - 2.0
                    c1, s1_ = (twice - 1.0) * c0, (twice + 1.0) * s0
                    c2, s2_ = twice * c1 - c0, twice * s1_ - s0
                    c3, s3 = twice * c2 - c1, twice * s2_ - s1_
                    cb, sb = c3 * c0 - s3 * s0, s3 * c0 + c3 * s0
                    cp, sp, cb, sb = (v.astype(BF16) for v in (cp, sp, cb, sb))
                    cc, ss, sc, cs = cp * cb, sp * sb, sp * cb, cp * sb
                    dst = pl.ds(pl.multiple_of(i * 512 + h * ROWS, ROWS), ROWS)
                    values = (cc + ss, sc - cs, cc - ss, sc + cs, c0, c1, c2, c3, s0, s1_, s2_, s3)
                    for n, v in enumerate(values):
                        state[n, dst, :] = v.astype(BF16)
                return 0

            lax.fori_loop(start, stop, block, 0)

        setup1 = functools.partial(setup, state1, air_ref, column1, 3.0)
        setup2 = functools.partial(setup, state2, obs_ref, column2, 4.0)
        pl.semaphore_wait(barrier, len(peers))

        x_sends = [
            send(part.at[(x + d) % 4], recv_x.at[d - 1], sx.at[d - 1], rx.at[d - 1], x_peer(d)) for d in (2, 1, 3)
        ]
        for s in x_sends:
            s.start()
        for d in (2, 6):
            pl.semaphore_signal(relay, inc=1, device_id=z_peer(d), device_id_type=MESH)

        for fetch in fetches[1:]:
            fetch.wait()
        columns(column1, src_ref)
        setup1(0, CUT[0])

        for s in x_sends:
            s.wait_recv()
        row = lax.broadcasted_iota(jnp.int32, (64, LANES), 0)
        even = row % 2 == 0
        total = part[x] + recv_x[0] + recv_x[1] + recv_x[2]
        quarter = ((row_freq(row) + 1) * blade_ref[...]) & 3
        cos_q = (quarter == 0).astype(F32) - (quarter == 2).astype(F32)
        sin_q = (quarter == 1).astype(F32) - (quarter == 3).astype(F32)
        turned = total * cos_q + swapped(total, even) * jnp.where(even, sin_q, -sin_q)
        own[...] = turned.reshape(2, 32, LANES)
        z_sends = [
            send(own.at[z_of(d) // 4], recv_z.at[z], sz.at[d - 1], rz.at[d - 1], z_peer(d))
            for d in (4, 3, 5, 2, 6, 1, 7)
        ]
        pl.semaphore_wait(relay, 2)
        for s in z_sends:
            s.start()
        recv_z[z] = own[zh]

        setup1(CUT[0], 8)
        columns(column2, air_ref)
        setup2(0, CUT[1])

        def radiate(line, state, mine, recv, ssem, rsem, near, beside):
            row = lax.broadcasted_iota(jnp.int32, (32, LANES), 0)
            even = row % 2 == 0
            side = jnp.where((row // 2) % 2 == 0, 1.0, -1.0).astype(F32)
            for zz in range(4):
                v = line(zz)
                hi = v.astype(BF16).astype(F32)
                kinds = []
                for piece in (hi, v - hi):
                    sw = swapped(piece, even)
                    sw = jnp.where(even, sw, -sw)
                    kinds.append((piece, piece * -side, sw, sw * side))
                for kind in range(4):
                    for jj in range(4):
                        pair = jnp.concatenate([q[kind][8 * jj : 8 * jj + 8] for q in kinds], axis=0)
                        lane = kind * 256 + (zz % 2) * LANES
                        weights[zz // 2, jj, :, lane : lane + LANES] = pair.astype(BF16)
            low = lax.broadcasted_iota(jnp.int32, (8, LANES), 0) < 4

            def copy(i):
                return send(mine.at[i], recv.at[i], ssem.at[i], rsem.at[i], (fi, block_panel(i)))

            def block(i, _):
                acc = [jnp.zeros((16, 256), F32)] * 4
                near_acc = jnp.zeros((64, LANES), F32)
                for kt in range(2):
                    rows = pl.ds(pl.multiple_of(i * 512 + kt * 256, 256), 256)
                    ec0, es0, ec1, es1 = (state[n, rows, :] for n in range(4))
                    for jj in range(4):
                        cj, sj = state[4 + jj, rows, :], state[8 + jj, rows, :]
                        big = jnp.concatenate(
                            [
                                jnp.concatenate([ec0 * cj, ec1 * cj], axis=1),
                                jnp.concatenate([es0 * sj, es1 * sj], axis=1),
                                jnp.concatenate([es0 * cj, es1 * cj], axis=1),
                                jnp.concatenate([ec0 * sj, ec1 * sj], axis=1),
                            ],
                            axis=0,
                        )
                        acc[jj] = acc[jj] + jnp.dot(weights[kt, jj], big, preferred_element_type=F32)
                    if near:
                        left = jnp.concatenate([weights[kt, jj, :, 0:256] for jj in range(4)], axis=0)
                        near_acc = near_acc + jnp.dot(left, hits[rows, :], preferred_element_type=F32)
                for jj in range(4):
                    both = acc[jj][0:8] + acc[jj][8:16]
                    out = jnp.where(low, both[:, :LANES], both[:, LANES:])
                    if near:
                        out = out + near_acc[16 * jj : 16 * jj + 8] + near_acc[16 * jj + 8 : 16 * jj + 16]
                    mine[i, 8 * jj : 8 * jj + 8, :] = out

                @pl.when(i < 7)
                def _():
                    copy(i).start()

                return 0

            lax.fori_loop(0, 8, block, 0)
            beside()
            copies = [copy(i) for i in range(7)]
            total = mine[7]
            for i in range(7):
                copies[i].wait_recv()
                total = total + recv[i]
            return total, copies

        def count(i, _):
            at = pl.multiple_of(block_panel(i) * LANES, LANES)
            near = [near_ref[n : n + 1, pl.ds(at, LANES)] - (y * 2 + c) * LANES for n in range(4)]
            index = lax.broadcasted_iota(jnp.int32, (LANES, LANES), 0).astype(F32).astype(BF16)
            half, none = jnp.asarray(0.5, BF16), jnp.asarray(0.0, BF16)
            for zz in range(4):
                total = None
                for n in range(4):
                    local = near[n] - zz * 8 * LANES
                    local = jnp.where((local >= 0) & (local < LANES), local, -1).astype(F32).astype(BF16)
                    found = jnp.where(index == local, half, none)
                    total = found if total is None else total + found
                hits[pl.ds(pl.multiple_of(i * 512 + zz * LANES, LANES), LANES), :] = total
            return 0

        def tail1():
            lax.fori_loop(0, 8, count, 0)
            setup2(CUT[1], CUT[2])

        for s in z_sends:
            s.wait_recv()
        incident, sends1 = radiate(lambda zz: recv_z[zz] + recv_z[zz + 4], state1, mine1, recv1, s1, r1, False, tail1)
        line2[zl] = incident * reflect_ref[...]
        l_sends = [
            send(line2.at[zl], line2.at[zl], sl.at[d - 1], rl.at[d - 1], line_peer(d)) for d in (2, 1, 3)
        ]
        for s in l_sends:
            s.start()

        setup2(CUT[2], 8)


        for s in l_sends:
            s.wait_recv()
        observed, sends2 = radiate(lambda zz: line2[zz], state2, mine2, recv2, s2, r2, True, lambda: None)
        spec[fi] = observed

        f_sends = [
            send(spec.at[fi], spec.at[fi], sf.at[d - 1], rf.at[d - 1], ((fi + d) % 8, pi)) for d in range(1, 8)
        ]
        for s in f_sends:
            s.start()

        def back_rows(i, _):
            col = lax.broadcasted_iota(jnp.int32, (32, 256), 1)
            t = lax.broadcasted_iota(jnp.int32, (32, 256), 0) + fi * T_DEV + i * 32
            m = (col // 32) * F_DEV + row_freq(col) + 1
            value = turn_cos(m * t + 1024 * (col % 2))
            hi = value.astype(BF16)
            dst = pl.ds(pl.multiple_of(i * 32, 32), 32)
            back_hi[dst, :] = hi
            back_lo[dst, :] = (value - hi.astype(F32)).astype(BF16)
            return 0

        lax.fori_loop(0, T_DEV // 32, back_rows, 0)
        for s in f_sends:
            s.wait_recv()

        seen = spec[...].reshape(256, LANES) * (1.0 / 16.0)
        hi = seen.astype(BF16)
        lo = (seen - hi.astype(F32)).astype(BF16)
        seen_ref[...] = jnp.concatenate([hi, lo], axis=1)

        for s in x_sends + z_sends + sends1 + l_sends + sends2 + f_sends:
            s.wait_send()

    pl.run_scoped(
        work,
        pltpu.VMEM((256, T_DEV), BF16),
        pltpu.VMEM((12, 4096, LANES), BF16),
        pltpu.VMEM((12, 4096, LANES), BF16),
        pltpu.VMEM((4096, LANES), BF16),
        pltpu.VMEM((4, 3, LANES, LANES), F32),
        pltpu.VMEM((4, 3, LANES, LANES), F32),
        pltpu.VMEM((2, 4, 16, 1024), BF16),
    )


def back(seen_ref, hi_ref, lo_ref, out_ref, made, done):
    copies = []
    for q in range(4):
        rows = pl.ds(q * LANES, LANES)
        wide = jnp.dot(hi_ref[rows, :], seen_ref[...], preferred_element_type=F32)
        narrow = jnp.dot(lo_ref[rows, :], seen_ref[:, :LANES], preferred_element_type=F32)
        made[rows, :] = wide[:, :LANES] + wide[:, LANES:] + narrow
        copies.append(pltpu.make_async_copy(made.at[rows], out_ref.at[rows], done.at[q]))
        copies[q].start()
    for copy in copies:
        copy.wait()


def on_device(load, blade, source, airframe, reflect, observer, near):
    args = (load, blade.reshape(1, LANES), source, airframe, reflect.reshape(1, LANES), observer, near.T)
    args = tuple(pltpu.with_memory_space_constraint(a, pltpu.HBM) for a in args)
    vmem = pl.BlockSpec(memory_space=pltpu.VMEM)
    dma = pltpu.SemaphoreType.DMA
    slots = [(4, 64), (3, 64), (2, 32), (8, 32), (8, 32), (7, 32), (4, 32), (8, 32), (7, 32), (8, 32)]
    scratch = [pltpu.VMEM(a.shape, a.dtype) for a in args] + [dma((7,)), pltpu.SemaphoreType.REGULAR]
    scratch += [pltpu.VMEM((*slot, LANES), F32) for slot in slots]
    scratch += [dma((n,)) for n in (3, 3, 7, 7, 7, 7, 3, 3, 7, 7, 7, 7)]
    shapes = ((256, 256), (T_DEV, 256), (T_DEV, 256))
    parts = pl.pallas_call(
        body,
        out_shape=[jax.ShapeDtypeStruct(s, BF16) for s in shapes],
        in_specs=[pl.BlockSpec(memory_space=pltpu.HBM)] * 7,
        out_specs=[vmem] * 3,
        scratch_shapes=scratch,
        compiler_params=pltpu.CompilerParams(
            collective_id=0, has_side_effects=True, vmem_limit_bytes=40 * 1024 * 1024
        ),
        name="rotor",
    )(*args)
    return pl.pallas_call(
        back,
        out_shape=jax.ShapeDtypeStruct((T_DEV, LANES), F32),
        in_specs=[vmem] * 3,
        out_specs=pl.BlockSpec(memory_space=pl.ANY),
        scratch_shapes=[pltpu.VMEM((T_DEV, LANES), F32), dma((4,))],
        compiler_params=pltpu.CompilerParams(vmem_limit_bytes=4 * 1024 * 1024),
        name="back",
    )(*parts)


def solution(mesh):
    return jax.shard_map(
        on_device,
        mesh=mesh,
        in_specs=(P("freq", "panel"), P("panel"), P(), P(), P("panel"), P(), P()),
        out_specs=P("freq", "panel"),
        check_vma=False,
    )
```
